32 devices in a mesh: row: 4 (over y, x), col: 8 (over z, core).
Axes of the slice: x: 2, y: 2, z: 4, core: 2. Of those that a mesh axis runs over, the one named last changes fastest.
Arguments:
- velocity: float32 [3, 4, 256, 1024], P(None, None, 'row', 'col'), may hold values from -6 to 6
- stress: float32 [6, 4, 256, 1024], P(None, None, 'row', 'col'), may hold values from -6 to 6
- buoyancy: float32 [4, 256, 1024], P(None, 'row', 'col'), may hold values from 0.2 to 0.4
- lame: float32 [4, 256, 1024], P(None, 'row', 'col'), may hold values from 0.08 to 0.2
- shear: float32 [4, 256, 1024], P(None, 'row', 'col'), may hold values from 0.08 to 0.2
- kernel: bfloat16 [12, 3, 2, 1024, 256], P(None, None, None, ('row', 'col')), may hold values from -1.1953125 to 1.1953125
- history: bfloat16 [11, 3, 2, 1024, 256], P(None, None, None, ('row', 'col')), may hold values from -6 to 6
Outputs:
- new_velocity: float32 [3, 4, 256, 1024], P(None, None, 'row', 'col')
- new_stress: float32 [6, 4, 256, 1024], P(None, None, 'row', 'col')
- spectra: float32 [2, 3, 2, 1024, 256], P(None, None, None, ('row', 'col'))
The draws below stay inside these ranges and needn't reach their ends.
All inputs are finite; a program needn't handle non-finite values.
Results may differ from the reference program's by a relative error of at most 0.0003.
Values sent between devices are 32-bit elements; how exact they have to be, the bound alone decides.
No kernel may reach another device: no remote copies, remote signals or barrier semaphores. Data moves between devices by JAX's collectives and lax.ppermute only.
A program may use at most 128 MiB of HBM per device.

```python
import math
import jax
import jax.numpy as jnp

LAYERS = 4
HIST = 12
STEPS = 2
NX = 256
NY = 1024


def shard_levels(stream_key, extent, split, least, high):
    factor_of, own = 1.0, jax.random.fold_in(stream_key, 6)
    for axis_at, blocks in split:
        heights = jnp.exp(jax.random.uniform(jax.random.fold_in(own, axis_at), (blocks,), jnp.float32, least / len(split), high / len(split)))
        factor_of = factor_of * jnp.repeat(heights, extent[axis_at] // blocks).reshape([-1 if axis == axis_at else 1 for axis in range(len(extent))])
    return factor_of


def centred(own_key, dims, deviation, bound, cuts=(), dtype=jnp.bfloat16):
    values = deviation * jax.random.normal(own_key, dims, jnp.float32)
    if cuts:
        values = values * shard_levels(own_key, dims, cuts, -0.22, 0.18)
    return jnp.clip(values, -bound, bound).astype(dtype)


def setup_inputs(seed: int = 0) -> dict:
    splits = jax.random.split(jax.random.key(seed), 8)
    velocity = centred(splits[0], (3, LAYERS, NX, NY), 1.0, 6.0, ((2, 4), (3, 8)), jnp.float32)
    stress = centred(splits[1], (6, LAYERS, NX, NY), 1.0, 6.0, ((2, 4), (3, 8)), jnp.float32)
    buoyancy = jnp.clip(jnp.exp(math.log(0.4) - 0.6931472 * jax.random.uniform(splits[2], (LAYERS, NX, NY), jnp.float32) ** shard_levels(splits[2], (LAYERS, NX, NY), ((1, 4), (2, 8)), -0.2, 0.2)), 0.2, 0.4)
    lame = jnp.clip(jnp.exp(math.log(0.2) - 0.91629077 * jax.random.uniform(splits[3], (LAYERS, NX, NY), jnp.float32) ** shard_levels(splits[3], (LAYERS, NX, NY), ((1, 4), (2, 8)), -0.2, 0.2)), 0.08, 0.2)
    shear = jnp.clip(jnp.exp(math.log(0.2) - 0.91629077 * jax.random.uniform(splits[4], (LAYERS, NX, NY), jnp.float32) ** shard_levels(splits[4], (LAYERS, NX, NY), ((1, 4), (2, 8)), -0.2, 0.2)), 0.08, 0.2)
    kernel = centred(splits[5], (HIST, 3, 2, NY, NX), 0.2, 1.1953125, ((3, 32),))
    history = centred(splits[6], (HIST - 1, 3, 2, NY, NX), 1.0, 6.0, ((3, 32),))
    return dict(velocity=velocity, stress=stress, buoyancy=buoyancy, lame=lame, shear=shear, kernel=kernel, history=history)


near_weight = 2.0 / 3.0
far_weight = -1.0 / 12.0


def plane_deriv(values, along_dim):
    return near_weight * (jnp.roll(values, -1, along_dim) - jnp.roll(values, 1, along_dim)) + far_weight * (jnp.roll(values, -2, along_dim) - jnp.roll(values, 2, along_dim))


def depth_deriv(values):
    layers = values.shape[1]
    padded = jnp.pad(values, ((0, 0), (2, 2), (0, 0), (0, 0)))
    return near_weight * (padded[:, 3:layers + 3] - padded[:, 1:layers + 1]) + far_weight * (padded[:, 4:layers + 4] - padded[:, 0:layers])


def complex_entry(source, index):
    return source[index, :, 0].astype(jnp.float32) + 1j * source[index, :, 1].astype(jnp.float32)


def update_stress(stress, grad_x, grad_y, grad_z, lame, shear, traction):
    diverge = grad_x[0] + grad_y[1] + grad_z[2]
    result = jnp.stack((
        stress[0] + lame * diverge + 2.0 * shear * grad_x[0],
        stress[1] + lame * diverge + 2.0 * shear * grad_y[1],
        stress[2] + lame * diverge + 2.0 * shear * grad_z[2],
        stress[3] + shear * (grad_y[0] + grad_x[1]),
        stress[4] + shear * (grad_z[0] + grad_x[2]),
        stress[5] + shear * (grad_z[1] + grad_y[2])))
    result = result.at[2, 0].add(traction[2])
    result = result.at[4, 0].add(traction[0])
    return result.at[5, 0].add(traction[1])


def reference(velocity, stress, buoyancy, lame, shear, kernel, history):
    earlier = []
    for step_index in range(STEPS):
        along_x = plane_deriv(jnp.stack((stress[0], stress[3], stress[4])), 2)
        along_y = plane_deriv(jnp.stack((stress[3], stress[1], stress[5])), 3)
        along_z = depth_deriv(jnp.stack((stress[4], stress[5], stress[2])))
        velocity = velocity + buoyancy * (along_x + along_y + along_z)
        spectrum = jnp.transpose(jnp.fft.fft2(velocity[:, 0], norm="ortho"), (0, 2, 1))
        total = complex_entry(kernel, 0) * spectrum
        for lag in range(1, HIST):
            if lag - 1 < len(earlier):
                source = earlier[lag - 1]
            else:
                source = complex_entry(history, lag - 1 - len(earlier))
            total = total + complex_entry(kernel, lag) * source
        traction = jnp.real(jnp.fft.ifft2(jnp.transpose(total, (0, 2, 1)), norm="ortho"))
        grad_x = plane_deriv(velocity, 2)
        grad_y = plane_deriv(velocity, 3)
        grad_z = depth_deriv(velocity)
        stress = update_stress(stress, grad_x, grad_y, grad_z, lame, shear, traction)
        earlier = [spectrum] + earlier
    spectra = jnp.stack([jnp.stack((jnp.real(entry), jnp.imag(entry)), axis=1) for entry in reversed(earlier)])
    return velocity, stress, spectra
```

```python
import functools
import math

import jax
import jax.numpy as jnp
from jax import lax
from jax.experimental import pallas as pl
from jax.experimental.pallas import tpu as pltpu
from jax.sharding import PartitionSpec as P

STEPS = 2
VMEM_LIMIT = 16 * 1024 * 1024
NEAR = 2.0 / 3.0
FAR = -1.0 / 12.0
F32 = jnp.float32
BF16 = jnp.bfloat16
NN = (((1,), (0,)), ((), ()))
NT = (((1,), (1,)), ((), ()))


def call(body, name, outs, *args, scratch=(), alias=None, flops=0):
    nbytes = sum(a.size * a.dtype.itemsize for a in args) + sum(
        math.prod(s) * jnp.dtype(d).itemsize for s, d in outs
    )
    results = pl.pallas_call(
        body,
        name=name,
        out_shape=[jax.ShapeDtypeStruct(s, d) for s, d in outs],
        in_specs=[
            pl.BlockSpec(memory_space=pltpu.SMEM if a.dtype == jnp.int32 else pltpu.VMEM)
            for a in args
        ],
        out_specs=[pl.BlockSpec(memory_space=pltpu.VMEM) for _ in outs],
        scratch_shapes=list(scratch),
        input_output_aliases=alias or {},
        compiler_params=pltpu.CompilerParams(vmem_limit_bytes=VMEM_LIMIT),
        cost_estimate=pl.CostEstimate(flops=flops, bytes_accessed=nbytes, transcendentals=0),
    )(*args)
    return list(results)


def split(x):
    hi = x.astype(BF16)
    return hi, (x - hi.astype(F32)).astype(BF16)


def dot3(a, b, dims):
    a_hi, a_lo = a
    b_hi, b_lo = b

    def one(u, v):
        return lax.dot_general(u, v, dims, preferred_element_type=F32)

    return one(a_hi, b_hi) + (one(a_lo, b_hi) + one(a_hi, b_lo))


def dot6(a, b, dims):
    return lax.dot_general(
        a, b, dims, precision=lax.Precision.HIGHEST, preferred_element_type=F32
    )


def iota(shape, dim):
    return lax.broadcasted_iota(jnp.int32, shape, dim)


def shift_perm(x, axis, shift):
    count = lax.axis_size(axis)
    return lax.ppermute(x, axis, [(i, (i + shift) % count) for i in range(count)])


def partner_perm(x):
    count = lax.axis_size("col")
    return lax.ppermute(x, "col", [(i, i ^ 1) for i in range(count)])


def tables(where, dims):
    rows, cols, xb, yb, kyb = dims
    nx, ny = rows * xb, cols * yb
    depth = cols // 2
    nk = rows * kyb

    def unit(phase, modulus):
        angle = (phase & (modulus - 1)).astype(F32) * (2.0 * math.pi / modulus)
        return jnp.cos(angle), jnp.sin(angle)

    def body(where_ref, oh, ol, ph, pl_, wh, wl):
        r, c = where_ref[0], where_ref[1]

        def put(hi_ref, lo_ref, index, value):
            hi, lo = split(value)
            hi_ref[index] = hi
            lo_ref[index] = lo

        for flip, hi_ref, lo_ref in ((0, oh, ol), (1, ph, pl_)):
            col = c ^ 1 if flip else c
            line = iota((nk, yb), 0)
            lane = iota((nk, yb), 1)
            wave = ((line // kyb + r) & (rows - 1)) * (cols * kyb) + col * kyb + line % kyb
            base_cos, base_sin = unit(wave * lane, ny)
            start = ((c - 2 * lane) & (cols - 1)) * yb
            turn_cos, turn_sin = unit(wave * start, ny)
            scale = 1.0 / math.sqrt(ny)
            for t in range(depth):
                tc, ts = turn_cos[:, t : t + 1] * scale, turn_sin[:, t : t + 1] * scale
                span = pl.ds(t * yb, yb)
                put(hi_ref, lo_ref, (pl.ds(0, nk), span), base_cos * tc - base_sin * ts)
                put(hi_ref, lo_ref, (pl.ds(nk, nk), span), -(base_sin * tc + base_cos * ts))
        base_cos, base_sin = unit(iota((xb, nx), 0) * iota((xb, nx), 1), nx)
        tall = max(8, rows)
        start = ((r - iota((tall, nx), 0)) & (rows - 1)) * xb
        turn_cos, turn_sin = unit(start * iota((tall, nx), 1), nx)
        scale = 1.0 / math.sqrt(nx)
        for s in range(rows):
            tc, ts = turn_cos[s : s + 1] * scale, turn_sin[s : s + 1] * scale
            cos = base_cos * tc - base_sin * ts
            sin = base_sin * tc + base_cos * ts
            top, low = pl.ds(2 * s * xb, xb), pl.ds((2 * s + 1) * xb, xb)
            put(wh, wl, (top, pl.ds(0, nx)), cos)
            put(wh, wl, (top, pl.ds(nx, nx)), -sin)
            put(wh, wl, (low, pl.ds(0, nx)), sin)
            put(wh, wl, (low, pl.ds(nx, nx)), cos)

    y_shape, x_shape = (2 * nk, depth * yb), (2 * nx, 2 * nx)
    outs = [(y_shape, BF16)] * 4 + [(x_shape, BF16)] * 2
    oh, ol, ph, pl_, wh, wl = call(body, "tables", outs, where)
    return (oh, ol), (ph, pl_), (wh, wl)


def past_sums(kernel, history):
    lags, comps, _, kyb, nx = kernel.shape

    def body(k_ref, h_ref, *out_refs):
        for comp in range(comps):
            line = pl.ds(comp * kyb, kyb)
            totals = [[None, None] for _ in range(STEPS)]
            for lag in range(1, lags):
                kr = k_ref[lag, comp, 0].astype(F32)
                ki = k_ref[lag, comp, 1].astype(F32)
                for step in range(STEPS):
                    if lag - 1 < step:
                        continue
                    hr = h_ref[lag - 1 - step, comp, 0].astype(F32)
                    hi = h_ref[lag - 1 - step, comp, 1].astype(F32)
                    for part, value in enumerate((kr * hr - ki * hi, kr * hi + ki * hr)):
                        old = totals[step][part]
                        totals[step][part] = value if old is None else old + value
            for step in range(STEPS):
                for part in range(2):
                    out_refs[step][line, pl.ds(part * nx, nx)] = totals[step][part]

    return call(body, "past", [((comps * kyb, 2 * nx), F32)] * STEPS, kernel, history)


ROW_PARTS = (0, 3, 4)
COL_PARTS = (3, 1, 5)


def edge_weights(yb):
    line, lane = iota((8, yb), 0), iota((8, yb), 1)
    target = jnp.where(line < 2, line, yb - 4 + line)
    return jnp.where((lane == target) & (line < 4), 1.0, 0.0).astype(F32)


def inner_weights(yb):
    gap = iota((yb, yb), 0) - iota((yb, yb), 1)
    value = jnp.where(gap == 1, NEAR, 0.0) - jnp.where(gap == -1, NEAR, 0.0)
    return value + jnp.where(gap == 2, FAR, 0.0) - jnp.where(gap == -2, FAR, 0.0)


def outer_weights(yb):
    line, lane = iota((8, yb), 0), iota((8, yb), 1)
    left_gap = jnp.where((line == 2) | (line == 3), line - 4 - lane, 99)
    right_gap = jnp.where(line < 2, yb + line - lane, 99)

    def value(gap):
        near = jnp.where(gap == 1, NEAR, 0.0) - jnp.where(gap == -1, NEAR, 0.0)
        return near + jnp.where(gap == 2, FAR, 0.0) - jnp.where(gap == -2, FAR, 0.0)

    return value(left_gap), value(right_gap)


def put_borders(planes, row_planes, col_planes, edge_ref, first_ref, last_ref):
    xb, yb = planes(row_planes[0]).shape
    for j, which in enumerate(row_planes):
        plane = planes(which)
        first_ref[2 * j : 2 * j + 2, :] = plane[:2]
        last_ref[2 * j : 2 * j + 2, :] = plane[xb - 2 :]
    stacked = jnp.concatenate([planes(which) for which in col_planes], axis=0)
    edge_ref[...] = dot6(edge_weights(yb), stacked, NT)


def row_deriv(pad_ref, plane, above, below):
    xb = plane.shape[0]
    pad_ref[8 : 8 + xb, :] = plane
    pad_ref[6:8, :] = above
    pad_ref[8 + xb : 10 + xb, :] = below
    near = pad_ref[9 : 9 + xb, :] - pad_ref[7 : 7 + xb, :]
    far = pad_ref[10 : 10 + xb, :] - pad_ref[6 : 6 + xb, :]
    return NEAR * near + FAR * far


def col_deriv(stacked, left, right):
    yb = stacked.shape[1]
    left_w, right_w = outer_weights(yb)
    inner = dot6(stacked, inner_weights(yb), NN)
    return inner + (dot6(left.T, left_w, NN) + dot6(right.T, right_w, NN))


def depth_deriv(at, layer, layers):
    total = None
    for step, weight in ((1, NEAR), (-1, -NEAR), (2, FAR), (-2, -FAR)):
        if 0 <= layer + step < layers:
            term = weight * at(layer + step)
            total = term if total is None else total + term
    return total


def borders_shapes(layers, xb, yb):
    planes = 3 * layers
    return [((8, planes * xb), F32), ((2 * planes, yb), F32), ((2 * planes, yb), F32)]


def first_borders(stress):
    _, layers, xb, yb = stress.shape

    def body(s_ref, *outs):
        rows = [(p, l) for p in ROW_PARTS for l in range(layers)]
        cols = [(p, l) for p in COL_PARTS for l in range(layers)]
        put_borders(lambda w: s_ref[w[0], w[1]], rows, cols, *outs)

    return call(body, "borders", borders_shapes(layers, xb, yb), stress)


def exchange(borders):
    edge, first, last = borders
    above = shift_perm(last, "row", 1)
    below = shift_perm(first, "row", -1)
    left = shift_perm(edge, "col", 1)
    right = shift_perm(edge, "col", -1)
    return above, below, left, right


def push_velocity(velocity, stress, buoyancy, halo):
    comps, layers, xb, yb = velocity.shape

    def body(v_ref, s_ref, b_ref, up, dn, lf, rt, nv_ref, top_ref, edge, first, last, pad):
        stacked = jnp.concatenate(
            [s_ref[p, l] for p in COL_PARTS for l in range(layers)], axis=0
        )
        along_y = col_deriv(stacked, lf[...], rt[...])
        depth_parts = (4, 5, 2)
        for comp in range(comps):
            for layer in range(layers):
                j = comp * layers + layer
                pair = slice(2 * j, 2 * j + 2)
                force = row_deriv(pad.at[j], s_ref[ROW_PARTS[comp], layer], up[pair, :], dn[pair, :])
                force = force + along_y[j * xb : (j + 1) * xb]
                force = force + depth_deriv(lambda l: s_ref[depth_parts[comp], l], layer, layers)
                new = v_ref[comp, layer] + b_ref[layer] * force
                nv_ref[comp, layer] = new
                if layer == 0:
                    top_ref[comp * xb : (comp + 1) * xb, :] = new
        planes = [(c, l) for c in range(comps) for l in range(layers)]
        put_borders(lambda w: nv_ref[w[0], w[1]], planes, planes, edge, first, last)

    outs = [(velocity.shape, F32), ((comps * xb, yb), F32)] + borders_shapes(layers, xb, yb)
    nv, top, *borders = call(
        body, "push_velocity", outs, velocity, stress, buoyancy, *halo,
        scratch=[pltpu.VMEM((comps * layers, xb + 16, yb), F32)],
    )
    return nv, top, borders


def push_stress(stress, velocity, lame, shear, halo):
    comps, layers, xb, yb = velocity.shape

    def body(s_ref, v_ref, l_ref, m_ref, up, dn, lf, rt, ns_ref, pad):
        stacked = jnp.concatenate(
            [v_ref[c, l] for c in range(comps) for l in range(layers)], axis=0
        )
        along_y = col_deriv(stacked, lf[...], rt[...])
        for layer in range(layers):
            gx, gy, gz = [], [], []
            for comp in range(comps):
                j = comp * layers + layer
                pair = slice(2 * j, 2 * j + 2)
                gx.append(row_deriv(pad.at[j], v_ref[comp, layer], up[pair, :], dn[pair, :]))
                gy.append(along_y[j * xb : (j + 1) * xb])
                gz.append(depth_deriv(lambda l: v_ref[comp, l], layer, layers))
            lam, mu = l_ref[layer], m_ref[layer]
            spread = lam * (gx[0] + gy[1] + gz[2])
            twice = 2.0 * mu
            ns_ref[0, layer] = s_ref[0, layer] + spread + twice * gx[0]
            ns_ref[1, layer] = s_ref[1, layer] + spread + twice * gy[1]
            ns_ref[2, layer] = s_ref[2, layer] + spread + twice * gz[2]
            ns_ref[3, layer] = s_ref[3, layer] + mu * (gy[0] + gx[1])
            ns_ref[4, layer] = s_ref[4, layer] + mu * (gz[0] + gx[2])
            ns_ref[5, layer] = s_ref[5, layer] + mu * (gz[1] + gy[2])

    return call(
        body, "push_stress", [(stress.shape, F32)], stress, velocity, lame, shear, *halo,
        scratch=[pltpu.VMEM((comps * layers, xb + 16, yb), F32)],
    )[0]


def add_traction(stress, pieces, with_borders):
    _, layers, xb, yb = stress.shape

    def body(s_ref, *refs):
        count = len(pieces)
        ns_ref, *outs = refs[count:]
        total = refs[0][...]
        for ref in refs[1:count]:
            total = total + ref[...]
        ns_ref[...] = s_ref[...]
        for comp, part in enumerate((4, 5, 2)):
            ns_ref[part, 0] = s_ref[part, 0] + total[comp * xb : (comp + 1) * xb]
        if with_borders:
            rows = [(p, l) for p in ROW_PARTS for l in range(layers)]
            cols = [(p, l) for p in COL_PARTS for l in range(layers)]
            put_borders(lambda w: ns_ref[w[0], w[1]], rows, cols, *outs)

    outs = [(stress.shape, F32)] + (borders_shapes(layers, xb, yb) if with_borders else [])
    new, *borders = call(body, "traction", outs, stress, *pieces)
    return new, borders


def part_forward(blocks, table, dims, name):
    rows, cols, xb, yb, kyb = dims
    nk = rows * kyb
    comps = blocks[0].shape[0] // xb

    def body(*refs):
        hi, lo, out = refs[-3:]
        data = jnp.concatenate([ref[...] for ref in refs[:-3]], axis=1)
        total = dot3((hi[...], lo[...]), split(data), NT)
        for s in range(rows):
            for comp in range(comps):
                lane = slice(comp * xb, (comp + 1) * xb)
                real = total[s * kyb : (s + 1) * kyb, lane]
                imag = total[nk + s * kyb : nk + (s + 1) * kyb, lane]
                at = (s * comps + comp) * kyb
                out[at : at + kyb, :] = jnp.concatenate([real, imag], axis=1)

    return call(body, name, [((rows * comps * kyb, 2 * xb), F32)], *blocks, *table)[0]


def join(mine, other, dims):
    rows = dims[0]
    height = mine.shape[0] // rows

    def body(a_ref, b_ref, *outs):
        for s, out in enumerate(outs):
            span = slice(s * height, (s + 1) * height)
            out[...] = a_ref[span, :] + b_ref[span, :]

    return call(body, "join", [((height, mine.shape[1]), F32)] * rows, mine, other)


def convolve(blocks, table, past, kernel, before, dims):
    rows, cols, xb, yb, kyb = dims
    nx = rows * xb
    comps = blocks[0].shape[0] // kyb
    step = len(before)

    def body(*refs):
        ins, outs = refs[: rows + 4 + step], refs[rows + 4 + step :]
        wide = (ins[rows][...], ins[rows + 1][...])
        past_ref, k_ref, olds = ins[rows + 2], ins[rows + 3], ins[rows + 4 :]
        data = jnp.concatenate([ref[...] for ref in ins[:rows]], axis=1)
        spec = dot3(split(data), wide, NN)
        spec_ref = outs[0]
        loads = []
        for comp in range(comps):
            line = slice(comp * kyb, (comp + 1) * kyb)
            now = (spec[line, :nx], spec[line, nx:])
            if step == STEPS - 1:
                for n in range(step):
                    spec_ref[n, comp] = olds[n][comp]
                spec_ref[step, comp, 0] = now[0]
                spec_ref[step, comp, 1] = now[1]
            else:
                spec_ref[comp, 0] = now[0]
                spec_ref[comp, 1] = now[1]
            real, imag = past_ref[line, :nx], past_ref[line, nx:]
            terms = [now] + [(old[comp, 0], old[comp, 1]) for old in reversed(olds)]
            for lag, (sr, si) in enumerate(terms):
                kr, ki = k_ref[lag, comp, 0].astype(F32), k_ref[lag, comp, 1].astype(F32)
                real = real + (kr * sr - ki * si)
                imag = imag + (kr * si + ki * sr)
            loads.append(jnp.concatenate([real, imag], axis=1))
        back = dot3(split(jnp.concatenate(loads, axis=0)), wide, NT)
        for s, out in enumerate(outs[1:]):
            out[...] = back[:, s * 2 * xb : (s + 1) * 2 * xb]

    one = (comps, 2, kyb, nx)
    spec_shape = (STEPS,) + one if step == STEPS - 1 else one
    outs = [(spec_shape, F32)] + [((comps * kyb, 2 * xb), F32)] * rows
    spec, *pieces = call(body, "convolve", outs, *blocks, *table, past, kernel, *before)
    return spec, pieces


def turn(blocks, dims):
    rows, cols, xb, yb, kyb = dims
    comps = blocks[0].shape[0] // kyb

    def body(*refs):
        out = refs[-1]
        for comp in range(comps):
            line = slice(comp * kyb, (comp + 1) * kyb)
            flat = jnp.concatenate([ref[line, :] for ref in refs[:-1]], axis=0).T
            out[comp * xb : (comp + 1) * xb, :] = jnp.concatenate([flat[:xb], flat[xb:]], axis=1)

    return call(body, "turn", [((comps * xb, 2 * rows * kyb), F32)], *blocks)[0]


def part_inverse(data, table, dims):
    cols, yb = dims[1], dims[3]

    def body(d_ref, hi, lo, out):
        out[...] = dot3(split(d_ref[...]), (hi[...], lo[...]), NN)

    shape = (data.shape[0], cols // 2 * yb)
    return call(body, "inverse_mine", [(shape, F32)], data, *table)[0]


def rest_inverse(mine, data, table, dims):
    cols, yb = dims[1], dims[3]

    def body(m_ref, d_ref, hi, lo, *outs):
        total = m_ref[...] + dot3(split(d_ref[...]), (hi[...], lo[...]), NN)
        for t, out in enumerate(outs):
            out[...] = total[:, t * yb : (t + 1) * yb]

    outs = [((data.shape[0], yb), F32)] * (cols // 2)
    return call(body, "inverse_other", outs, mine, data, *table)


def on_device(velocity, stress, buoyancy, lame, shear, kernel, history):
    rows, cols = lax.axis_size("row"), lax.axis_size("col")
    xb, yb = velocity.shape[2:]
    kyb = kernel.shape[3]
    dims = (rows, cols, xb, yb, kyb)
    where = jnp.stack([lax.axis_index("row"), lax.axis_index("col")]).astype(jnp.int32)

    halo = exchange(first_borders(stress))
    mine, other, wide = tables(where, dims)
    past = past_sums(kernel, history)
    recent = kernel[:STEPS]
    spectra = []
    for step in range(STEPS):
        velocity, top, borders = push_velocity(velocity, stress, buoyancy, halo)
        blocks = [top] + [shift_perm(top, "col", 2 * t) for t in range(1, cols // 2)]
        sent = part_forward(blocks, other, dims, "forward_other")
        came = partner_perm(sent)
        kept = part_forward(blocks, mine, dims, "forward_mine")
        pieces = join(kept, came, dims)
        pieces = pieces[:1] + [shift_perm(pieces[s], "row", s) for s in range(1, rows)]
        spec, pieces = convolve(pieces, wide, past[step], recent, spectra, dims)
        spectra.append(spec)
        pieces = pieces[:1] + [shift_perm(pieces[s], "row", -s) for s in range(1, rows)]
        flat = turn(pieces, dims)
        flat_other = partner_perm(flat)
        total = part_inverse(flat, mine, dims)
        pieces = rest_inverse(total, flat_other, other, dims)
        pieces = pieces[:1] + [shift_perm(pieces[t], "col", -2 * t) for t in range(1, cols // 2)]
        stress = push_stress(stress, velocity, lame, shear, exchange(borders))
        stress, borders = add_traction(stress, pieces, step < STEPS - 1)
        if step < STEPS - 1:
            halo = exchange(borders)
    return (velocity, stress, spectra[-1])


def solution(mesh):
    return jax.shard_map(
        on_device,
        mesh=mesh,
        in_specs=(
            P(None, None, "row", "col"),
            P(None, None, "row", "col"),
            P(None, "row", "col"),
            P(None, "row", "col"),
            P(None, "row", "col"),
            P(None, None, None, ("row", "col"), None),
            P(None, None, None, ("row", "col"), None),
        ),
        out_specs=(
            P(None, None, "row", "col"),
            P(None, None, "row", "col"),
            P(None, None, None, ("row", "col"), None),
        ),
        check_vma=False,
    )
```

```python
import functools
import math

import jax
import jax.numpy as jnp
from jax import lax
from jax.experimental import pallas as pl
from jax.experimental.pallas import tpu as pltpu
from jax.sharding import PartitionSpec as P

STEPS = 2
VMEM_LIMIT = 16 * 1024 * 1024
NEAR = 2.0 / 3.0
FAR = -1.0 / 12.0
F32 = jnp.float32
BF16 = jnp.bfloat16
NN = (((1,), (0,)), ((), ()))
NT = (((1,), (1,)), ((), ()))


def call(body, name, outs, *args, scratch=(), after=()):
    nbytes = sum(a.size * a.dtype.itemsize for a in args) + sum(
        math.prod(s) * jnp.dtype(d).itemsize for s, d in outs
    )
    count = len(args)

    def run(*refs):
        body(*refs[:count], *refs[count + len(after) :])

    results = pl.pallas_call(
        run,
        name=name,
        out_shape=[jax.ShapeDtypeStruct(s, d) for s, d in outs],
        in_specs=[
            pl.BlockSpec(memory_space=pltpu.SMEM if a.dtype == jnp.int32 else pltpu.VMEM)
            for a in args
        ]
        + [pl.BlockSpec(memory_space=pl.ANY) for _ in after],
        out_specs=[pl.BlockSpec(memory_space=pltpu.VMEM) for _ in outs],
        scratch_shapes=list(scratch),
        compiler_params=pltpu.CompilerParams(vmem_limit_bytes=VMEM_LIMIT),
        cost_estimate=pl.CostEstimate(flops=0, bytes_accessed=nbytes, transcendentals=0),
    )(*args, *after)
    return list(results)


def split(x):
    hi = x.astype(BF16)
    return hi, (x - hi.astype(F32)).astype(BF16)


def dot3(a, b, dims):
    a_hi, a_lo = a
    b_hi, b_lo = b

    def one(u, v):
        return lax.dot_general(u, v, dims, preferred_element_type=F32)

    return one(a_hi, b_hi) + (one(a_lo, b_hi) + one(a_hi, b_lo))


def dot6(a, b, dims):
    return lax.dot_general(
        a, b, dims, precision=lax.Precision.HIGHEST, preferred_element_type=F32
    )


def iota(shape, dim):
    return lax.broadcasted_iota(jnp.int32, shape, dim)


def shift_perm(x, axis, shift):
    count = lax.axis_size(axis)
    return lax.ppermute(x, axis, [(i, (i + shift) % count) for i in range(count)])


def partner_perm(x):
    count = lax.axis_size("col")
    return lax.ppermute(x, "col", [(i, i ^ 1) for i in range(count)])


def beyond(index, length):
    return jnp.where(index < 2, index - 2, index - 2 + length)


def tables(where, dims):
    rows, cols, xb, yb, kyb = dims
    nx, ny = rows * xb, cols * yb
    depth = cols // 2
    nk = rows * kyb

    def unit(phase, modulus):
        angle = (phase & (modulus - 1)).astype(F32) * (2.0 * math.pi / modulus)
        return jnp.cos(angle), jnp.sin(angle)

    def body(where_ref, oh, ol, ph, pl_, wh, wl, eo, ep, we):
        r, c = where_ref[0], where_ref[1]

        def put(hi_ref, lo_ref, index, value):
            hi, lo = split(value)
            hi_ref[index] = hi
            lo_ref[index] = lo

        for flip, hi_ref, lo_ref, side_ref in ((0, oh, ol, eo), (1, ph, pl_, ep)):
            col = c ^ 1 if flip else c
            line = iota((nk, yb), 0)
            lane = iota((nk, yb), 1)
            wave = ((line // kyb + r) & (rows - 1)) * (cols * kyb) + col * kyb + line % kyb
            base_cos, base_sin = unit(wave * lane, ny)
            start = ((c - 2 * lane) & (cols - 1)) * yb
            turn_cos, turn_sin = unit(wave * start, ny)
            scale = 1.0 / math.sqrt(ny)
            for t in range(depth):
                tc, ts = turn_cos[:, t : t + 1] * scale, turn_sin[:, t : t + 1] * scale
                span = pl.ds(t * yb, yb)
                put(hi_ref, lo_ref, (pl.ds(0, nk), span), base_cos * tc - base_sin * ts)
                put(hi_ref, lo_ref, (pl.ds(nk, nk), span), -(base_sin * tc + base_cos * ts))
            line, lane = iota((depth * 8, nk), 0), iota((depth * 8, nk), 1)
            wave = ((lane // kyb + r) & (rows - 1)) * (cols * kyb) + col * kyb + lane % kyb
            spot = ((c - 2 * (line // 8)) & (cols - 1)) * yb + beyond(line % 8, yb)
            side_cos, side_sin = unit(wave * spot, ny)
            side_ref[:, :nk] = side_cos * scale
            side_ref[:, nk:] = -side_sin * scale
        base_cos, base_sin = unit(iota((xb, nx), 0) * iota((xb, nx), 1), nx)
        tall = max(8, rows)
        start = ((r - iota((tall, nx), 0)) & (rows - 1)) * xb
        turn_cos, turn_sin = unit(start * iota((tall, nx), 1), nx)
        scale = 1.0 / math.sqrt(nx)
        for s in range(rows):
            tc, ts = turn_cos[s : s + 1] * scale, turn_sin[s : s + 1] * scale
            cos = base_cos * tc - base_sin * ts
            sin = base_sin * tc + base_cos * ts
            top, low = pl.ds(2 * s * xb, xb), pl.ds((2 * s + 1) * xb, xb)
            put(wh, wl, (top, pl.ds(0, nx)), cos)
            put(wh, wl, (top, pl.ds(nx, nx)), -sin)
            put(wh, wl, (low, pl.ds(0, nx)), sin)
            put(wh, wl, (low, pl.ds(nx, nx)), cos)
        line, lane = iota((rows * 8, nx), 0), iota((rows * 8, nx), 1)
        spot = ((r - line // 8) & (rows - 1)) * xb + beyond(line % 4, xb)
        cos, sin = unit(spot * lane, nx)
        real = line % 8 < 4
        we[:, :nx] = jnp.where(real, cos, sin) * scale
        we[:, nx:] = jnp.where(real, -sin, cos) * scale

    y_shape, x_shape = (2 * nk, depth * yb), (2 * nx, 2 * nx)
    outs = [(y_shape, BF16)] * 4 + [(x_shape, BF16)] * 2
    outs += [((depth * 8, 2 * nk), F32)] * 2 + [((rows * 8, 2 * nx), F32)]
    oh, ol, ph, pl_, wh, wl, eo, ep, we = call(body, "tables", outs, where)
    return (oh, ol), (ph, pl_), (wh, wl), (eo, ep, we)


def past_sums(kernel, history):
    lags, comps, _, kyb, nx = kernel.shape

    def body(k_ref, h_ref, *out_refs):
        for comp in range(comps):
            line = pl.ds(comp * kyb, kyb)
            totals = [[None, None] for _ in range(STEPS)]
            for lag in range(1, lags):
                kr = k_ref[lag, comp, 0].astype(F32)
                ki = k_ref[lag, comp, 1].astype(F32)
                for step in range(STEPS):
                    if lag - 1 < step:
                        continue
                    hr = h_ref[lag - 1 - step, comp, 0].astype(F32)
                    hi = h_ref[lag - 1 - step, comp, 1].astype(F32)
                    for part, value in enumerate((kr * hr - ki * hi, kr * hi + ki * hr)):
                        old = totals[step][part]
                        totals[step][part] = value if old is None else old + value
            for step in range(STEPS):
                for part in range(2):
                    out_refs[step][line, pl.ds(part * nx, nx)] = totals[step][part]

    return call(body, "past", [((comps * kyb, 2 * nx), F32)] * STEPS, kernel, history)


ROW_PARTS = (0, 3, 4)
COL_PARTS = (3, 1, 5)


def edge_weights(yb):
    line, lane = iota((8, yb), 0), iota((8, yb), 1)
    target = jnp.where(line < 2, line, yb - 4 + line)
    return jnp.where((lane == target) & (line < 4), 1.0, 0.0).astype(F32)


def inner_weights(yb):
    gap = iota((yb, yb), 0) - iota((yb, yb), 1)
    value = jnp.where(gap == 1, NEAR, 0.0) - jnp.where(gap == -1, NEAR, 0.0)
    return value + jnp.where(gap == 2, FAR, 0.0) - jnp.where(gap == -2, FAR, 0.0)


def outer_weights(yb):
    line, lane = iota((8, yb), 0), iota((8, yb), 1)
    left_gap = jnp.where((line == 2) | (line == 3), line - 4 - lane, 99)
    right_gap = jnp.where(line < 2, yb + line - lane, 99)

    def value(gap):
        near = jnp.where(gap == 1, NEAR, 0.0) - jnp.where(gap == -1, NEAR, 0.0)
        return near + jnp.where(gap == 2, FAR, 0.0) - jnp.where(gap == -2, FAR, 0.0)

    return value(left_gap), value(right_gap)


def put_borders(planes, row_planes, col_planes, edge_ref, first_ref, last_ref):
    xb, yb = planes(row_planes[0]).shape
    for j, which in enumerate(row_planes):
        plane = planes(which)
        first_ref[2 * j : 2 * j + 2, :] = plane[:2]
        last_ref[2 * j : 2 * j + 2, :] = plane[xb - 2 :]
    stacked = jnp.concatenate([planes(which) for which in col_planes], axis=0)
    edge_ref[...] = dot6(edge_weights(yb), stacked, NT)


def row_deriv(pad_ref, plane, above, below):
    xb = plane.shape[0]
    pad_ref[8 : 8 + xb, :] = plane
    pad_ref[6:8, :] = above
    pad_ref[8 + xb : 10 + xb, :] = below
    near = pad_ref[9 : 9 + xb, :] - pad_ref[7 : 7 + xb, :]
    far = pad_ref[10 : 10 + xb, :] - pad_ref[6 : 6 + xb, :]
    return NEAR * near + FAR * far


def col_deriv(stacked, left, right):
    yb = stacked.shape[1]
    left_w, right_w = outer_weights(yb)
    inner = dot6(stacked, inner_weights(yb), NN)
    return inner + (dot6(left.T, left_w, NN) + dot6(right.T, right_w, NN))


def depth_deriv(at, layer, layers):
    total = None
    for step, weight in ((1, NEAR), (-1, -NEAR), (2, FAR), (-2, -FAR)):
        if 0 <= layer + step < layers:
            term = weight * at(layer + step)
            total = term if total is None else total + term
    return total


def borders_shapes(layers, xb, yb):
    planes = 3 * layers
    return [((8, planes * xb), F32), ((2 * planes, yb), F32), ((2 * planes, yb), F32)]


def row_patch(above, below, xb):
    line, lane = iota((xb, 4), 0), iota((xb, 4), 1)
    gap = beyond(lane, xb) - line
    near = jnp.where(gap == 1, NEAR, 0.0) - jnp.where(gap == -1, NEAR, 0.0)
    weights = near + jnp.where(gap == 2, FAR, 0.0) - jnp.where(gap == -2, FAR, 0.0)
    total = weights[:, 0:1] * above[0:1] + weights[:, 1:2] * above[1:2]
    return total + (weights[:, 2:3] * below[0:1] + weights[:, 3:4] * below[1:2])


def plane_list(parts, layers):
    return [(p, l) for p in parts for l in range(layers)]


def first_borders(stress):
    _, layers, xb, yb = stress.shape

    def body(s_ref, *outs):
        rows, cols = plane_list(ROW_PARTS, layers), plane_list(COL_PARTS, layers)
        put_borders(lambda w: s_ref[w[0], w[1]], rows, cols, *outs)

    return call(body, "borders", borders_shapes(layers, xb, yb), stress)


def exchange_edges(edge):
    return shift_perm(edge, "col", 1), shift_perm(edge, "col", -1)


def exchange(borders):
    edge, first, last = borders
    above = shift_perm(last, "row", 1)
    below = shift_perm(first, "row", -1)
    return (above, below, *exchange_edges(edge))


DEPTH_PARTS = (4, 5, 2)


def push_inner(velocity, stress, buoyancy):
    comps, layers, xb, yb = velocity.shape

    def body(v_ref, s_ref, b_ref, nv_ref, pad):
        none = jnp.zeros((2, yb), F32)
        stacked = jnp.concatenate(
            [s_ref[p, l] for p, l in plane_list(COL_PARTS, layers)], axis=0
        )
        along_y = dot6(stacked, inner_weights(yb), NN)
        for comp in range(comps):
            for layer in range(layers):
                j = comp * layers + layer
                force = row_deriv(pad.at[j], s_ref[ROW_PARTS[comp], layer], none, none)
                force = force + along_y[j * xb : (j + 1) * xb]
                force = force + depth_deriv(lambda l: s_ref[DEPTH_PARTS[comp], l], layer, layers)
                nv_ref[comp, layer] = v_ref[comp, layer] + b_ref[layer] * force

    return call(
        body, "push_inner", [(velocity.shape, F32)], velocity, stress, buoyancy,
        scratch=[pltpu.VMEM((comps * layers, xb + 16, yb), F32)],
    )[0]


def push_top(inner, buoyancy, halo):
    comps, layers, xb, yb = inner.shape

    def body(v_ref, b_ref, up, dn, lf, rt, top_ref):
        left_w, right_w = outer_weights(yb)
        for comp in range(comps):
            j = comp * layers
            pair, lane = slice(2 * j, 2 * j + 2), slice(j * xb, (j + 1) * xb)
            patch = row_patch(up[pair, :], dn[pair, :], xb)
            patch = patch + dot6(lf[:, lane].T, left_w, NN) + dot6(rt[:, lane].T, right_w, NN)
            top_ref[comp * xb : (comp + 1) * xb, :] = v_ref[comp, 0] + b_ref[0] * patch

    return call(body, "push_top", [((comps * xb, yb), F32)], inner, buoyancy, *halo)[0]


def push_rest(inner, buoyancy, halo, top):
    comps, layers, xb, yb = inner.shape

    def body(v_ref, b_ref, up, dn, lf, rt, top_ref, nv_ref, edge, first, last):
        left_w, right_w = outer_weights(yb)
        along_y = dot6(lf[...].T, left_w, NN) + dot6(rt[...].T, right_w, NN)
        for comp in range(comps):
            nv_ref[comp, 0] = top_ref[comp * xb : (comp + 1) * xb, :]
            for layer in range(1, layers):
                j = comp * layers + layer
                pair = slice(2 * j, 2 * j + 2)
                patch = row_patch(up[pair, :], dn[pair, :], xb) + along_y[j * xb : (j + 1) * xb]
                nv_ref[comp, layer] = v_ref[comp, layer] + b_ref[layer] * patch
        planes = plane_list(range(comps), layers)
        put_borders(lambda w: nv_ref[w[0], w[1]], planes, planes, edge, first, last)

    outs = [(inner.shape, F32)] + borders_shapes(layers, xb, yb)
    new, *borders = call(body, "push_rest", outs, inner, buoyancy, *halo, top)
    return new, borders


def push_velocity(velocity, stress, buoyancy, halo):
    comps, layers, xb, yb = velocity.shape

    def body(v_ref, s_ref, b_ref, up, dn, lf, rt, nv_ref, top_ref, pad):
        stacked = jnp.concatenate(
            [s_ref[p, l] for p, l in plane_list(COL_PARTS, layers)], axis=0
        )
        along_y = col_deriv(stacked, lf[...], rt[...])
        for comp in range(comps):
            for layer in range(layers):
                j = comp * layers + layer
                pair = slice(2 * j, 2 * j + 2)
                force = row_deriv(pad.at[j], s_ref[ROW_PARTS[comp], layer], up[pair, :], dn[pair, :])
                force = force + along_y[j * xb : (j + 1) * xb]
                force = force + depth_deriv(lambda l: s_ref[DEPTH_PARTS[comp], l], layer, layers)
                new = v_ref[comp, layer] + b_ref[layer] * force
                nv_ref[comp, layer] = new
                if layer == 0 and comp < comps - 1:
                    top_ref[comp * xb : (comp + 1) * xb, :] = new

    outs = [(velocity.shape, F32), (((comps - 1) * xb, yb), F32)]
    return call(
        body, "push_velocity", outs, velocity, stress, buoyancy, *halo,
        scratch=[pltpu.VMEM((comps * layers, xb + 16, yb), F32)],
    )


def push_stress(stress, velocity, lame, shear, halo, traction=None):
    comps, layers, xb, yb = velocity.shape

    def body(s_ref, v_ref, l_ref, m_ref, up, dn, lf, rt, *refs):
        stacked = jnp.concatenate(
            [v_ref[c, l] for c, l in plane_list(range(comps), layers)], axis=0
        )
        if traction is None:
            ns_ref, *outs, pad = refs
        else:
            t_ref, ns_ref, pad = refs
        along_y = col_deriv(stacked, lf[...], rt[...])
        skip = up.shape[0] - 2 * comps * layers
        for layer in range(layers):
            gx, gy, gz = [], [], []
            for comp in range(comps):
                j = comp * layers + layer
                pair = slice(skip + 2 * j, skip + 2 * j + 2)
                gx.append(row_deriv(pad.at[j], v_ref[comp, layer], up[pair, :], dn[pair, :]))
                gy.append(along_y[j * xb : (j + 1) * xb])
                gz.append(depth_deriv(lambda l: v_ref[comp, l], layer, layers))
            lam, mu = l_ref[layer], m_ref[layer]
            spread = lam * (gx[0] + gy[1] + gz[2])
            twice = 2.0 * mu
            old = [s_ref[part, layer] for part in range(6)]
            if traction is not None and layer == 0:
                for comp, part in enumerate(DEPTH_PARTS):
                    old[part] = old[part] + t_ref[comp * xb : (comp + 1) * xb, :]
            ns_ref[0, layer] = old[0] + spread + twice * gx[0]
            ns_ref[1, layer] = old[1] + spread + twice * gy[1]
            ns_ref[2, layer] = old[2] + spread + twice * gz[2]
            ns_ref[3, layer] = old[3] + mu * (gy[0] + gx[1])
            ns_ref[4, layer] = old[4] + mu * (gz[0] + gx[2])
            ns_ref[5, layer] = old[5] + mu * (gz[1] + gy[2])
        if traction is None:
            rows, cols = plane_list(ROW_PARTS, layers), plane_list(COL_PARTS, layers)
            put_borders(lambda w: ns_ref[w[0], w[1]], rows, cols, *outs)

    args = [stress, velocity, lame, shear, *halo] + ([] if traction is None else [traction])
    outs = [(stress.shape, F32)] + (borders_shapes(layers, xb, yb) if traction is None else [])
    new, *borders = call(
        body, "push_stress", outs, *args,
        scratch=[pltpu.VMEM((comps * layers, xb + 16, yb), F32)],
    )
    return new, borders


def total_of(refs):
    total = refs[0][...]
    for ref in refs[1:]:
        total = total + ref[...]
    return total


def top_after(pieces, velocity, buoyancy):
    comps, layers, xb, yb = velocity.shape
    height = pieces[0].shape[0]

    def body(v_ref, b_ref, *refs):
        *piece_refs, sum_ref, face_ref, pad = refs
        total = total_of(piece_refs)
        sum_ref[...] = total
        main = comps * xb
        force = row_deriv(pad, total[:xb], total[main : main + 2], total[main + 2 : main + 4])
        side = total[main + 8 : main + 16, :xb].T
        line, lane = iota((8, yb), 0), iota((8, yb), 1)
        gap = jnp.where(line < 4, beyond(line, yb) - lane, 99)
        near = jnp.where(gap == 1, NEAR, 0.0) - jnp.where(gap == -1, NEAR, 0.0)
        outer = near + jnp.where(gap == 2, FAR, 0.0) - jnp.where(gap == -2, FAR, 0.0)
        force = force + (dot6(total[xb : 2 * xb], inner_weights(yb), NN) + dot6(side, outer, NN))
        face_ref[...] = v_ref[comps - 1, 0] + b_ref[0] * force

    return call(
        body, "top_after", [((height, yb), F32), ((xb, yb), F32)], velocity, buoyancy, *pieces,
        scratch=[pltpu.VMEM((xb + 16, yb), F32)],
    )


def finish_velocity(velocity, buoyancy, traction, face):
    comps, layers, xb, yb = velocity.shape

    def body(v_ref, b_ref, t_ref, f_ref, nv_ref, edge, first, last):
        for comp in range(comps):
            push = t_ref[comp * xb : (comp + 1) * xb, :]
            for layer in range(layers):
                new = v_ref[comp, layer]
                if layer == 0 and comp == comps - 1:
                    new = f_ref[...]
                if layer in (1, 2):
                    weight = -NEAR if layer == 1 else -FAR
                    new = new + b_ref[layer] * (weight * push)
                nv_ref[comp, layer] = new
        planes = plane_list(range(comps), layers)
        put_borders(lambda w: nv_ref[w[0], w[1]], planes, planes, edge, first, last)

    outs = [(velocity.shape, F32)] + borders_shapes(layers, xb, yb)
    new, *borders = call(body, "finish_velocity", outs, velocity, buoyancy, traction, face)
    return new, borders


def add_traction(stress, pieces):
    xb = stress.shape[2]

    def body(s_ref, *refs):
        *piece_refs, ns_ref = refs
        total = total_of(piece_refs)
        ns_ref[...] = s_ref[...]
        for comp, part in enumerate(DEPTH_PARTS):
            ns_ref[part, 0] = s_ref[part, 0] + total[comp * xb : (comp + 1) * xb]

    return call(body, "traction", [(stress.shape, F32)], stress, *pieces)[0]


def part_forward(groups, table, dims, name, after=()):
    rows, cols, xb, yb, kyb = dims
    nk = rows * kyb
    comps = sum(blocks[0].shape[0] for blocks in groups) // xb
    depth = cols // 2

    def body(*refs):
        hi, lo, out = refs[-3:]
        data = jnp.concatenate(
            [
                jnp.concatenate([ref[...] for ref in refs[g * depth : (g + 1) * depth]], axis=1)
                for g in range(len(groups))
            ],
            axis=0,
        )
        total = dot3((hi[...], lo[...]), split(data), NT)
        for s in range(rows):
            for comp in range(comps):
                lane = slice(comp * xb, (comp + 1) * xb)
                real = total[s * kyb : (s + 1) * kyb, lane]
                imag = total[nk + s * kyb : nk + (s + 1) * kyb, lane]
                at = (s * comps + comp) * kyb
                out[at : at + kyb, :] = jnp.concatenate([real, imag], axis=1)

    blocks = [block for group in groups for block in group]
    return call(body, name, [((rows * comps * kyb, 2 * xb), F32)], *blocks, *table, after=after)[0]


def join(mine, other, first, last, dims, after):
    rows = dims[0]
    height, extra = mine.shape[0] // rows, first.shape[0]
    riders = {1: 1, rows - 1: 0}

    def body(a_ref, b_ref, *refs):
        borders, outs = refs[:2], refs[2:]
        for s, out in enumerate(outs):
            span = slice(s * height, (s + 1) * height)
            out[:height, :] = a_ref[span, :] + b_ref[span, :]
            if s in riders:
                out[height:, :] = borders[riders[s]][...]

    outs = [((height + (extra if s in riders else 0), mine.shape[1]), F32) for s in range(rows)]
    return call(body, "join", outs, mine, other, first, last, after=after)


def convolve(blocks, table, past, kernel, before, dims, side=None):
    rows, cols, xb, yb, kyb = dims
    nx = rows * xb
    comps = blocks[0].shape[0] // kyb
    step = len(before)

    def body(*refs):
        if side is not None:
            side_ref, *refs = refs
        ins, outs = refs[: rows + 4 + step], refs[rows + 4 + step :]
        wide = (ins[rows][...], ins[rows + 1][...])
        past_ref, k_ref, olds = ins[rows + 2], ins[rows + 3], ins[rows + 4 :]
        data = jnp.concatenate([ref[: comps * kyb, :] for ref in ins[:rows]], axis=1)
        spec = dot3(split(data), wide, NN)
        spec_ref = outs[0]
        loads = []
        for comp in range(comps):
            line = slice(comp * kyb, (comp + 1) * kyb)
            now = (spec[line, :nx], spec[line, nx:])
            if step == STEPS - 1:
                for n in range(step):
                    spec_ref[n, comp] = olds[n][comp]
                spec_ref[step, comp, 0] = now[0]
                spec_ref[step, comp, 1] = now[1]
            else:
                spec_ref[comp, 0] = now[0]
                spec_ref[comp, 1] = now[1]
            real, imag = past_ref[line, :nx], past_ref[line, nx:]
            terms = [now] + [(old[comp, 0], old[comp, 1]) for old in reversed(olds)]
            for lag, (sr, si) in enumerate(terms):
                kr, ki = k_ref[lag, comp, 0].astype(F32), k_ref[lag, comp, 1].astype(F32)
                real = real + (kr * sr - ki * si)
                imag = imag + (kr * si + ki * sr)
            loads.append(jnp.concatenate([real, imag], axis=1))
        back = dot3(split(jnp.concatenate(loads, axis=0)), wide, NT)
        if side is not None:
            halo = dot6(side_ref[...], loads[0], NT)
        for s, out in enumerate(outs[1:]):
            out[: comps * kyb, :] = back[:, s * 2 * xb : (s + 1) * 2 * xb]
            if side is not None:
                out[comps * kyb :, :] = jnp.zeros((8, 2 * xb), F32)
                out[comps * kyb :, :kyb] = halo[8 * s : 8 * s + 8]

    one = (comps, 2, kyb, nx)
    spec_shape = (STEPS,) + one if step == STEPS - 1 else one
    height = comps * kyb + (0 if side is None else 8)
    outs = [(spec_shape, F32)] + [((height, 2 * xb), F32)] * rows
    args = ([] if side is None else [side]) + [*blocks, *table, past, kernel, *before]
    spec, *pieces = call(body, "convolve", outs, *args)
    return spec, pieces


def turn(blocks, dims, comps, after):
    rows, cols, xb, yb, kyb = dims
    main, wide = comps * xb, 2 * rows * kyb
    sides = blocks[0].shape[0] > comps * kyb

    def body(*refs):
        *blocks, out = refs
        for comp in range(comps):
            line = slice(comp * kyb, (comp + 1) * kyb)
            flat = jnp.concatenate([ref[line, :] for ref in blocks], axis=0).T
            out[comp * xb : (comp + 1) * xb, :] = jnp.concatenate([flat[:xb], flat[xb:]], axis=1)
        if sides:
            low = comps * kyb
            parts = [ref[low + 4 * p : low + 4 * p + 4, :kyb] for p in range(2) for ref in blocks]
            out[main : main + 8, :] = jnp.zeros((8, wide), F32)
            out[main : main + 4, :] = jnp.concatenate(parts, axis=1)

    return call(body, "turn", [((main + (8 if sides else 0), wide), F32)], *blocks, after=after)[0]


def y_inverse(d_ref, hi, lo, dims, side_ref):
    xb, yb, depth = dims[2], dims[3], dims[1] // 2
    total = dot3(split(d_ref[...]), (hi[...], lo[...]), NN)
    if side_ref is None:
        return total
    beside = dot6(side_ref[...], d_ref[xb : 2 * xb, :], NT)
    gap = jnp.zeros((8, yb - xb), F32)
    parts = [jnp.concatenate([beside[8 * t : 8 * t + 8], gap], axis=1) for t in range(depth)]
    return jnp.concatenate([total, jnp.concatenate(parts, axis=1)], axis=0)


def part_inverse(data, table, dims, side=None):
    def body(d_ref, hi, lo, *refs):
        out = refs[-1]
        out[...] = y_inverse(d_ref, hi, lo, dims, refs[0] if side is not None else None)

    shape = (data.shape[0] + (0 if side is None else 8), dims[1] // 2 * dims[3])
    extra = [] if side is None else [side]
    return call(body, "inverse_mine", [(shape, F32)], data, *table, *extra)[0]


def rest_inverse(mine, data, table, dims, side=None):
    cols, yb = dims[1], dims[3]

    def body(m_ref, d_ref, hi, lo, *refs):
        side_ref, outs = (None, refs) if side is None else (refs[0], refs[1:])
        total = m_ref[...] + y_inverse(d_ref, hi, lo, dims, side_ref)
        for t, out in enumerate(outs):
            out[...] = total[:, t * yb : (t + 1) * yb]

    outs = [((mine.shape[0], yb), F32)] * (cols // 2)
    extra = [] if side is None else [side]
    return call(body, "inverse_other", outs, mine, data, *table, *extra)


def gather_depth(block):
    count = lax.axis_size("col") // 2
    return [block] + [shift_perm(block, "col", 2 * t) for t in range(1, count)]


def forward(groups, borders, tables_, dims):
    mine, other = tables_[:2]
    edge, first, last = borders
    sent = part_forward(groups, other, dims, "forward_other", after=(first,))
    came = partner_perm(sent)
    kept = part_forward(groups, mine, dims, "forward_mine")
    beside = exchange_edges(edge)
    pieces = join(kept, came, first, last, dims, beside)
    pieces = pieces[:1] + [shift_perm(pieces[s], "row", s) for s in range(1, dims[0])]
    return pieces, (pieces[1], pieces[-1], *beside)


def inverse(pieces, tables_, dims, comps, last, token):
    mine, other, _, (side_mine, side_other, _) = tables_
    rows, cols = dims[:2]
    pieces = pieces[:1] + [shift_perm(pieces[s], "row", -s) for s in range(1, rows)]
    flat = turn(pieces, dims, comps, (token,))
    flat_other = partner_perm(flat)
    total = part_inverse(flat, mine, dims, None if last else side_mine)
    pieces = rest_inverse(total, flat_other, other, dims, None if last else side_other)
    return pieces[:1] + [shift_perm(pieces[t], "col", -2 * t) for t in range(1, cols // 2)]


def on_device(velocity, stress, buoyancy, lame, shear, kernel, history):
    rows, cols = lax.axis_size("row"), lax.axis_size("col")
    xb, yb = velocity.shape[2:]
    kyb = kernel.shape[3]
    dims = (rows, cols, xb, yb, kyb)
    where = jnp.stack([lax.axis_index("row"), lax.axis_index("col")]).astype(jnp.int32)

    halo = exchange(first_borders(stress))
    inner = push_inner(velocity, stress, buoyancy)
    top = push_top(inner, buoyancy, halo)
    faces = gather_depth(top)
    tables_ = tables(where, dims)
    past = past_sums(kernel, history)
    recent = kernel[:STEPS]
    velocity, borders = push_rest(inner, buoyancy, halo, top)
    spectra = []
    groups = [faces]
    traction = None
    for step in range(STEPS):
        last = step == STEPS - 1
        pieces, halo = forward(groups, borders, tables_, dims)
        side = None if last else tables_[3][2]
        spec, pieces = convolve(pieces, tables_[2], past[step], recent, spectra, dims, side)
        spectra.append(spec)
        stress, next_borders = push_stress(stress, velocity, lame, shear, halo, traction)
        token = stress if last else next_borders[1]
        pieces = inverse(pieces, tables_, dims, recent.shape[1], last, token)
        if last:
            break
        velocity, early = push_velocity(velocity, stress, buoyancy, exchange(next_borders))
        groups = [gather_depth(early)]
        traction, face = top_after(pieces, velocity, buoyancy)
        groups.append(gather_depth(face))
        velocity, borders = finish_velocity(velocity, buoyancy, traction, face)
    stress = add_traction(stress, pieces)
    return (velocity, stress, spectra[-1])


def solution(mesh):
    return jax.shard_map(
        on_device,
        mesh=mesh,
        in_specs=(
            P(None, None, "row", "col"),
            P(None, None, "row", "col"),
            P(None, "row", "col"),
            P(None, "row", "col"),
            P(None, "row", "col"),
            P(None, None, None, ("row", "col"), None),
            P(None, None, None, ("row", "col"), None),
        ),
        out_specs=(
            P(None, None, "row", "col"),
            P(None, None, "row", "col"),
            P(None, None, None, ("row", "col"), None),
        ),
        check_vma=False,
    )
```

```python
import math

import jax
import jax.numpy as jnp
from jax import lax
from jax.experimental import pallas as pl
from jax.experimental.pallas import tpu as pltpu
from jax.sharding import PartitionSpec as P


STEPS = 2
VMEM_LIMIT = 16 * 1024 * 1024
NEAR = 2.0 / 3.0
FAR = -1.0 / 12.0
F32 = jnp.float32
BF16 = jnp.bfloat16
NN = (((1,), (0,)), ((), ()))
NT = (((1,), (1,)), ((), ()))


def call(body, outs, *args, scratch=(), after=()):
    nbytes = sum(a.size * a.dtype.itemsize for a in args) + sum(
        math.prod(s) * jnp.dtype(d).itemsize for s, d in outs
    )
    count = len(args)

    def run(*refs):
        body(*refs[:count], *refs[count + len(after) :])

    results = pl.pallas_call(
        run,
        out_shape=[jax.ShapeDtypeStruct(s, d) for s, d in outs],
        in_specs=[
            pl.BlockSpec(memory_space=pltpu.SMEM if a.dtype == jnp.int32 else pltpu.VMEM)
            for a in args
        ]
        + [pl.BlockSpec(memory_space=pl.ANY) for _ in after],
        out_specs=[pl.BlockSpec(memory_space=pltpu.VMEM) for _ in outs],
        scratch_shapes=list(scratch),
        compiler_params=pltpu.CompilerParams(vmem_limit_bytes=VMEM_LIMIT),
        cost_estimate=pl.CostEstimate(flops=0, bytes_accessed=nbytes, transcendentals=0),
    )(*args, *after)
    return list(results)


def split(x):
    hi = x.astype(BF16)
    return hi, (x - hi.astype(F32)).astype(BF16)


def dot3(a, b, dims):
    a_hi, a_lo = a
    b_hi, b_lo = b

    def one(u, v):
        return lax.dot_general(u, v, dims, preferred_element_type=F32)

    return one(a_hi, b_hi) + (one(a_lo, b_hi) + one(a_hi, b_lo))


def dot6(a, b, dims):
    return lax.dot_general(
        a, b, dims, precision=lax.Precision.HIGHEST, preferred_element_type=F32
    )


def iota(shape, dim):
    return lax.broadcasted_iota(jnp.int32, shape, dim)


def shift_perm(x, axis, shift):
    count = lax.axis_size(axis)
    return lax.ppermute(x, axis, [(i, (i + shift) % count) for i in range(count)])


def depth_mask(t, odd, depth):
    return (depth - t) & (depth - 1) if odd else t


def depth_perm(x, t):
    count = lax.axis_size("col")
    return lax.ppermute(
        x, "col", [(i, i ^ (2 * depth_mask(t, i & 1, count // 2))) for i in range(count)]
    )


def partner_perm(x):
    count = lax.axis_size("col")
    return lax.ppermute(x, "col", [(i, i ^ 1) for i in range(count)])


def beyond(index, length):
    return jnp.where(index < 2, index - 2, index - 2 + length)


def tables(where, dims):
    rows, cols, xb, yb, kyb = dims
    nx, ny = rows * xb, cols * yb
    depth = cols // 2
    nk = rows * kyb

    def unit(phase, modulus):
        angle = (phase & (modulus - 1)).astype(F32) * (2.0 * math.pi / modulus)
        return jnp.cos(angle), jnp.sin(angle)

    def body(where_ref, oh, ol, ph, pl_, wh, wl, eo, ep, we):
        r, c = where_ref[0], where_ref[1]

        def met(t):
            turned = jnp.where((c & 1) == 1, (depth - t) & (depth - 1), t & (depth - 1))
            return c ^ (2 * turned)

        def put(hi_ref, lo_ref, index, value):
            hi, lo = split(value)
            hi_ref[index] = hi
            lo_ref[index] = lo

        line = iota((nk, yb), 0)
        lane = iota((nk, yb), 1)
        first_wave = ((line // kyb + r) & (rows - 1)) * (cols * kyb) + c * kyb + line % kyb
        own_cos, own_sin = unit(first_wave * lane, ny)
        hop = ((c ^ 1) - c) * kyb
        hop_cos, hop_sin = unit(hop * iota((8, yb), 1), ny)
        hop_cos, hop_sin = hop_cos[0:1], hop_sin[0:1]
        for flip, hi_ref, lo_ref, side_ref in ((0, oh, ol, eo), (1, ph, pl_, ep)):
            col = c ^ 1 if flip else c
            base_cos, base_sin = own_cos, own_sin
            if flip:
                base_cos = own_cos * hop_cos - own_sin * hop_sin
                base_sin = own_sin * hop_cos + own_cos * hop_sin
            turn = iota((max(8, depth), nk), 0)
            across = iota((max(8, depth), nk), 1)
            wave = ((across // kyb + r) & (rows - 1)) * (cols * kyb) + col * kyb + across % kyb
            turn_cos, turn_sin = unit(wave * ((met(turn)) * yb), ny)
            turn_cos, turn_sin = turn_cos.T, turn_sin.T
            scale = 1.0 / math.sqrt(ny)
            for t in range(depth):
                tc, ts = turn_cos[:, t : t + 1] * scale, turn_sin[:, t : t + 1] * scale
                span = pl.ds(t * yb, yb)
                put(hi_ref, lo_ref, (pl.ds(0, nk), span), base_cos * tc - base_sin * ts)
                put(hi_ref, lo_ref, (pl.ds(nk, nk), span), -(base_sin * tc + base_cos * ts))
            line, lane = iota((depth * 8, nk), 0), iota((depth * 8, nk), 1)
            wave = ((lane // kyb + r) & (rows - 1)) * (cols * kyb) + col * kyb + lane % kyb
            spot = (met(line // 8)) * yb + beyond(line % 8, yb)
            side_cos, side_sin = unit(wave * spot, ny)
            side_ref[:, :nk] = side_cos * scale
            side_ref[:, nk:] = -side_sin * scale
        base_cos, base_sin = unit(iota((xb, nx), 0) * iota((xb, nx), 1), nx)
        tall = max(8, rows)
        start = ((r - iota((tall, nx), 0)) & (rows - 1)) * xb
        turn_cos, turn_sin = unit(start * iota((tall, nx), 1), nx)
        scale = 1.0 / math.sqrt(nx)
        for s in range(rows):
            tc, ts = turn_cos[s : s + 1] * scale, turn_sin[s : s + 1] * scale
            cos = base_cos * tc - base_sin * ts
            sin = base_sin * tc + base_cos * ts
            top, low = pl.ds(2 * s * xb, xb), pl.ds((2 * s + 1) * xb, xb)
            put(wh, wl, (top, pl.ds(0, nx)), cos)
            put(wh, wl, (top, pl.ds(nx, nx)), -sin)
            put(wh, wl, (low, pl.ds(0, nx)), sin)
            put(wh, wl, (low, pl.ds(nx, nx)), cos)
        line, lane = iota((rows * 8, nx), 0), iota((rows * 8, nx), 1)
        spot = ((r - line // 8) & (rows - 1)) * xb + beyond(line % 4, xb)
        cos, sin = unit(spot * lane, nx)
        real = line % 8 < 4
        we[:, :nx] = jnp.where(real, cos, sin) * scale
        we[:, nx:] = jnp.where(real, -sin, cos) * scale

    y_shape, x_shape = (2 * nk, depth * yb), (2 * nx, 2 * nx)
    outs = [(y_shape, BF16)] * 4 + [(x_shape, BF16)] * 2
    outs += [((depth * 8, 2 * nk), F32)] * 2 + [((rows * 8, 2 * nx), F32)]
    oh, ol, ph, pl_, wh, wl, eo, ep, we = call(body, outs, where)
    return (oh, ol), (ph, pl_), (wh, wl), (eo, ep, we)


def past_sums(kernel, history):
    lags, comps, _, kyb, nx = kernel.shape

    def body(k_ref, h_ref, *out_refs):
        for comp in range(comps):
            line = pl.ds(comp * kyb, kyb)
            totals = [[None, None] for _ in range(STEPS)]
            for lag in range(1, lags):
                kr = k_ref[lag, comp, 0].astype(F32)
                ki = k_ref[lag, comp, 1].astype(F32)
                for step in range(STEPS):
                    if lag - 1 < step:
                        continue
                    hr = h_ref[lag - 1 - step, comp, 0].astype(F32)
                    hi = h_ref[lag - 1 - step, comp, 1].astype(F32)
                    for part, value in enumerate((kr * hr - ki * hi, kr * hi + ki * hr)):
                        old = totals[step][part]
                        totals[step][part] = value if old is None else old + value
            for step in range(STEPS):
                for part in range(2):
                    out_refs[step][line, pl.ds(part * nx, nx)] = totals[step][part]

    return call(body, [((comps * kyb, 2 * nx), F32)] * STEPS, kernel, history)


ROW_PARTS = (0, 3, 4)
COL_PARTS = (3, 1, 5)


def edge_weights(yb):
    line, lane = iota((8, yb), 0), iota((8, yb), 1)
    target = jnp.where(line < 2, line, yb - 4 + line)
    return jnp.where((lane == target) & (line < 4), 1.0, 0.0).astype(F32)


def inner_weights(yb):
    gap = iota((yb, yb), 0) - iota((yb, yb), 1)
    value = jnp.where(gap == 1, NEAR, 0.0) - jnp.where(gap == -1, NEAR, 0.0)
    return value + jnp.where(gap == 2, FAR, 0.0) - jnp.where(gap == -2, FAR, 0.0)


def outer_weights(yb):
    line, lane = iota((8, yb), 0), iota((8, yb), 1)
    left_gap = jnp.where((line == 2) | (line == 3), line - 4 - lane, 99)
    right_gap = jnp.where(line < 2, yb + line - lane, 99)

    def value(gap):
        near = jnp.where(gap == 1, NEAR, 0.0) - jnp.where(gap == -1, NEAR, 0.0)
        return near + jnp.where(gap == 2, FAR, 0.0) - jnp.where(gap == -2, FAR, 0.0)

    return value(left_gap), value(right_gap)


def put_borders(planes, row_planes, col_planes, edge_ref, first_ref, last_ref):
    xb, yb = planes(row_planes[0]).shape
    for j, which in enumerate(row_planes):
        plane = planes(which)
        first_ref[2 * j : 2 * j + 2, :] = plane[:2]
        last_ref[2 * j : 2 * j + 2, :] = plane[xb - 2 :]
    stacked = jnp.concatenate([planes(which) for which in col_planes], axis=0)
    edge_ref[...] = dot6(edge_weights(yb), stacked, NT)


def row_deriv(pad_ref, plane, above, below):
    xb = plane.shape[0]
    pad_ref[8 : 8 + xb, :] = plane
    pad_ref[6:8, :] = above
    pad_ref[8 + xb : 10 + xb, :] = below
    near = pad_ref[9 : 9 + xb, :] - pad_ref[7 : 7 + xb, :]
    far = pad_ref[10 : 10 + xb, :] - pad_ref[6 : 6 + xb, :]
    return NEAR * near + FAR * far


def col_deriv(stacked, left, right):
    yb = stacked.shape[1]
    left_w, right_w = outer_weights(yb)
    inner = dot6(stacked, inner_weights(yb), NN)
    return inner + (dot6(left.T, left_w, NN) + dot6(right.T, right_w, NN))


def depth_deriv(at, layer, layers):
    total = None
    for step, weight in ((1, NEAR), (-1, -NEAR), (2, FAR), (-2, -FAR)):
        if 0 <= layer + step < layers:
            term = weight * at(layer + step)
            total = term if total is None else total + term
    return total


def borders_shapes(layers, xb, yb):
    planes = 3 * layers
    return [((8, planes * xb), F32), ((2 * planes, yb), F32), ((2 * planes, yb), F32)]


def row_patch(above, below, xb):
    line, lane = iota((xb, 4), 0), iota((xb, 4), 1)
    gap = beyond(lane, xb) - line
    near = jnp.where(gap == 1, NEAR, 0.0) - jnp.where(gap == -1, NEAR, 0.0)
    weights = near + jnp.where(gap == 2, FAR, 0.0) - jnp.where(gap == -2, FAR, 0.0)
    total = weights[:, 0:1] * above[0:1] + weights[:, 1:2] * above[1:2]
    return total + (weights[:, 2:3] * below[0:1] + weights[:, 3:4] * below[1:2])


def plane_list(parts, layers):
    return [(p, l) for p in parts for l in range(layers)]


def first_borders(stress):
    _, layers, xb, yb = stress.shape

    def body(s_ref, *outs):
        rows, cols = plane_list(ROW_PARTS, layers), plane_list(COL_PARTS, layers)
        put_borders(lambda w: s_ref[w[0], w[1]], rows, cols, *outs)

    return call(body, borders_shapes(layers, xb, yb), stress)


def exchange_edges(edge):
    return shift_perm(edge, "col", 1), shift_perm(edge, "col", -1)


def exchange(borders):
    edge, first, last = borders
    above = shift_perm(last, "row", 1)
    below = shift_perm(first, "row", -1)
    return (above, below, *exchange_edges(edge))


DEPTH_PARTS = (4, 5, 2)


def inner_force(stress, comps):
    _, layers, xb, yb = stress.shape

    def body(s_ref, f_ref, pad):
        none = jnp.zeros((2, yb), F32)
        stacked = jnp.concatenate(
            [s_ref[p, l] for p, l in plane_list(COL_PARTS, layers)], axis=0
        )
        along_y = dot6(stacked, inner_weights(yb), NN)
        for comp in range(comps):
            for layer in range(layers):
                j = comp * layers + layer
                force = row_deriv(pad.at[j], s_ref[ROW_PARTS[comp], layer], none, none)
                force = force + along_y[j * xb : (j + 1) * xb]
                force = force + depth_deriv(lambda l: s_ref[DEPTH_PARTS[comp], l], layer, layers)
                f_ref[comp, layer] = force

    return call(
        body, [((comps, layers, xb, yb), F32)], stress,
        scratch=[pltpu.VMEM((comps * layers, xb + 16, yb), F32)],
    )[0]


def push_top(velocity, inner, buoyancy, halo):
    comps, layers, xb, yb = inner.shape

    def body(v_ref, f_ref, b_ref, up, dn, lf, rt, top_ref):
        left_w, right_w = outer_weights(yb)
        for comp in range(comps):
            j = comp * layers
            pair, lane = slice(2 * j, 2 * j + 2), slice(j * xb, (j + 1) * xb)
            patch = row_patch(up[pair, :], dn[pair, :], xb)
            patch = patch + dot6(lf[:, lane].T, left_w, NN) + dot6(rt[:, lane].T, right_w, NN)
            push = b_ref[0] * (f_ref[comp, 0] + patch)
            top_ref[comp * xb : (comp + 1) * xb, :] = v_ref[comp, 0] + push

    return call(body, [((comps * xb, yb), F32)], velocity, inner, buoyancy, *halo)[0]


def push_rest(velocity, inner, buoyancy, halo, top):
    comps, layers, xb, yb = inner.shape

    def body(v_ref, f_ref, b_ref, up, dn, lf, rt, top_ref, nv_ref, edge, first, last):
        left_w, right_w = outer_weights(yb)
        along_y = dot6(lf[...].T, left_w, NN) + dot6(rt[...].T, right_w, NN)
        for comp in range(comps):
            nv_ref[comp, 0] = top_ref[comp * xb : (comp + 1) * xb, :]
            for layer in range(1, layers):
                j = comp * layers + layer
                pair = slice(2 * j, 2 * j + 2)
                patch = row_patch(up[pair, :], dn[pair, :], xb) + along_y[j * xb : (j + 1) * xb]
                push = b_ref[layer] * (f_ref[comp, layer] + patch)
                nv_ref[comp, layer] = v_ref[comp, layer] + push
        planes = plane_list(range(comps), layers)
        put_borders(lambda w: nv_ref[w[0], w[1]], planes, planes, edge, first, last)

    outs = [(inner.shape, F32)] + borders_shapes(layers, xb, yb)
    new, *borders = call(body, outs, velocity, inner, buoyancy, *halo, top)
    return new, borders


def push_velocity(velocity, stress, buoyancy, halo):
    comps, layers, xb, yb = velocity.shape

    def body(v_ref, s_ref, b_ref, up, dn, lf, rt, nv_ref, pad):
        stacked = jnp.concatenate(
            [s_ref[p, l] for p, l in plane_list(COL_PARTS, layers)], axis=0
        )
        along_y = col_deriv(stacked, lf[...], rt[...])
        for comp in range(comps):
            for layer in range(layers):
                j = comp * layers + layer
                pair = slice(2 * j, 2 * j + 2)
                force = row_deriv(pad.at[j], s_ref[ROW_PARTS[comp], layer], up[pair, :], dn[pair, :])
                force = force + along_y[j * xb : (j + 1) * xb]
                force = force + depth_deriv(lambda l: s_ref[DEPTH_PARTS[comp], l], layer, layers)
                nv_ref[comp, layer] = v_ref[comp, layer] + b_ref[layer] * force

    return call(
        body, [(velocity.shape, F32)], velocity, stress, buoyancy, *halo,
        scratch=[pltpu.VMEM((comps * layers, xb + 16, yb), F32)],
    )[0]


def push_stress(stress, velocity, lame, shear, halo, traction=None):
    comps, layers, xb, yb = velocity.shape

    def body(s_ref, v_ref, l_ref, m_ref, up, dn, lf, rt, *refs):
        stacked = jnp.concatenate(
            [v_ref[c, l] for c, l in plane_list(range(comps), layers)], axis=0
        )
        if traction is None:
            ns_ref, *outs, pad = refs
        else:
            t_ref, ns_ref, pad = refs
        along_y = col_deriv(stacked, lf[...], rt[...])
        skip = up.shape[0] - 2 * comps * layers
        for layer in range(layers):
            gx, gy, gz = [], [], []
            for comp in range(comps):
                j = comp * layers + layer
                pair = slice(skip + 2 * j, skip + 2 * j + 2)
                gx.append(row_deriv(pad.at[j], v_ref[comp, layer], up[pair, :], dn[pair, :]))
                gy.append(along_y[j * xb : (j + 1) * xb])
                gz.append(depth_deriv(lambda l: v_ref[comp, l], layer, layers))
            lam, mu = l_ref[layer], m_ref[layer]
            spread = lam * (gx[0] + gy[1] + gz[2])
            twice = 2.0 * mu
            old = [s_ref[part, layer] for part in range(6)]
            if traction is not None and layer == 0:
                for comp, part in enumerate(DEPTH_PARTS):
                    old[part] = old[part] + t_ref[comp * xb : (comp + 1) * xb, :]
            ns_ref[0, layer] = old[0] + spread + twice * gx[0]
            ns_ref[1, layer] = old[1] + spread + twice * gy[1]
            ns_ref[2, layer] = old[2] + spread + twice * gz[2]
            ns_ref[3, layer] = old[3] + mu * (gy[0] + gx[1])
            ns_ref[4, layer] = old[4] + mu * (gz[0] + gx[2])
            ns_ref[5, layer] = old[5] + mu * (gz[1] + gy[2])
        if traction is None:
            rows, cols = plane_list(ROW_PARTS, layers), plane_list(COL_PARTS, layers)
            put_borders(lambda w: ns_ref[w[0], w[1]], rows, cols, *outs)

    args = [stress, velocity, lame, shear, *halo] + ([] if traction is None else [traction])
    outs = [(stress.shape, F32)] + (borders_shapes(layers, xb, yb) if traction is None else [])
    new, *borders = call(
        body, outs, *args,
        scratch=[pltpu.VMEM((comps * layers, xb + 16, yb), F32)],
    )
    return new, borders


def total_of(refs):
    total = refs[0][...]
    for ref in refs[1:]:
        total = total + ref[...]
    return total


def top_after(pieces, velocity, buoyancy):
    comps, _, xb, yb = velocity.shape
    height = pieces[0].shape[0]

    def body(v_ref, b_ref, *refs):
        *piece_refs, sum_ref, face_ref, pad = refs
        total = total_of(piece_refs)
        sum_ref[...] = total
        main = comps * xb
        force = row_deriv(pad, total[:xb], total[main : main + 2], total[main + 2 : main + 4])
        side = total[main + 8 : main + 16, :xb].T
        line, lane = iota((8, yb), 0), iota((8, yb), 1)
        gap = jnp.where(line < 4, beyond(line, yb) - lane, 99)
        near = jnp.where(gap == 1, NEAR, 0.0) - jnp.where(gap == -1, NEAR, 0.0)
        outer = near + jnp.where(gap == 2, FAR, 0.0) - jnp.where(gap == -2, FAR, 0.0)
        force = force + (dot6(total[xb : 2 * xb], inner_weights(yb), NN) + dot6(side, outer, NN))
        for comp in range(comps - 1):
            face_ref[comp * xb : (comp + 1) * xb, :] = v_ref[comp, 0]
        face_ref[(comps - 1) * xb :, :] = v_ref[comps - 1, 0] + b_ref[0] * force

    return call(
        body, [((height, yb), F32), ((comps * xb, yb), F32)], velocity, buoyancy, *pieces,
        scratch=[pltpu.VMEM((xb + 16, yb), F32)],
    )


def finish_velocity(velocity, buoyancy, traction, face):
    comps, layers, xb, yb = velocity.shape

    def body(v_ref, b_ref, t_ref, f_ref, nv_ref, edge, first, last):
        for comp in range(comps):
            push = t_ref[comp * xb : (comp + 1) * xb, :]
            for layer in range(layers):
                new = v_ref[comp, layer]
                if layer == 0 and comp == comps - 1:
                    new = f_ref[comp * xb :, :]
                if layer in (1, 2):
                    weight = -NEAR if layer == 1 else -FAR
                    new = new + b_ref[layer] * (weight * push)
                nv_ref[comp, layer] = new
        planes = plane_list(range(comps), layers)
        put_borders(lambda w: nv_ref[w[0], w[1]], planes, planes, edge, first, last)

    outs = [(velocity.shape, F32)] + borders_shapes(layers, xb, yb)
    new, *borders = call(body, outs, velocity, buoyancy, traction, face)
    return new, borders


def add_traction(stress, pieces):
    xb = stress.shape[2]

    def body(s_ref, *refs):
        *piece_refs, ns_ref = refs
        total = total_of(piece_refs)
        ns_ref[...] = s_ref[...]
        for comp, part in enumerate(DEPTH_PARTS):
            ns_ref[part, 0] = s_ref[part, 0] + total[comp * xb : (comp + 1) * xb]

    return call(body, [(stress.shape, F32)], stress, *pieces)[0]


def part_forward(blocks, table, dims, after=()):
    rows, _, xb, _, kyb = dims
    nk = rows * kyb
    comps = blocks[0].shape[0] // xb

    def body(*refs):
        hi, lo, out = refs[-3:]
        data = jnp.concatenate([ref[...] for ref in refs[:-3]], axis=1)
        total = dot3((hi[...], lo[...]), split(data), NT)
        for s in range(rows):
            for comp in range(comps):
                lane = slice(comp * xb, (comp + 1) * xb)
                real = total[s * kyb : (s + 1) * kyb, lane]
                imag = total[nk + s * kyb : nk + (s + 1) * kyb, lane]
                at = (s * comps + comp) * kyb
                out[at : at + kyb, :] = jnp.concatenate([real, imag], axis=1)

    return call(body, [((rows * comps * kyb, 2 * xb), F32)], *blocks, *table, after=after)[0]


def join(mine, other, first, last, dims):
    rows = dims[0]
    height, extra = mine.shape[0] // rows, first.shape[0]
    riders = {1: 1, rows - 1: 0}

    def body(a_ref, b_ref, *refs):
        borders, outs = refs[:2], refs[2:]
        for s, out in enumerate(outs):
            span = slice(s * height, (s + 1) * height)
            out[:height, :] = a_ref[span, :] + b_ref[span, :]
            if s in riders:
                out[height:, :] = borders[riders[s]][...]

    outs = [((height + (extra if s in riders else 0), mine.shape[1]), F32) for s in range(rows)]
    return call(body, outs, mine, other, first, last)


def convolve(blocks, table, past, kernel, before, dims, side=None):
    rows, _, xb, _, kyb = dims
    nx = rows * xb
    comps = blocks[0].shape[0] // kyb
    step = len(before)

    def body(*refs):
        if side is not None:
            side_ref, *refs = refs
        ins, outs = refs[: rows + 4 + step], refs[rows + 4 + step :]
        wide = (ins[rows][...], ins[rows + 1][...])
        past_ref, k_ref, olds = ins[rows + 2], ins[rows + 3], ins[rows + 4 :]
        data = jnp.concatenate([ref[: comps * kyb, :] for ref in ins[:rows]], axis=1)
        spec = dot3(split(data), wide, NN)
        spec_ref = outs[0]
        loads = []
        for comp in range(comps):
            line = slice(comp * kyb, (comp + 1) * kyb)
            now = (spec[line, :nx], spec[line, nx:])
            if step == STEPS - 1:
                for n in range(step):
                    spec_ref[n, comp] = olds[n][comp]
                spec_ref[step, comp, 0] = now[0]
                spec_ref[step, comp, 1] = now[1]
            else:
                spec_ref[comp, 0] = now[0]
                spec_ref[comp, 1] = now[1]
            real, imag = past_ref[line, :nx], past_ref[line, nx:]
            terms = [now] + [(old[comp, 0], old[comp, 1]) for old in reversed(olds)]
            for lag, (sr, si) in enumerate(terms):
                kr, ki = k_ref[lag, comp, 0].astype(F32), k_ref[lag, comp, 1].astype(F32)
                real = real + (kr * sr - ki * si)
                imag = imag + (kr * si + ki * sr)
            loads.append(jnp.concatenate([real, imag], axis=1))
        back = dot3(split(jnp.concatenate(loads, axis=0)), wide, NT)
        if side is not None:
            halo = dot6(side_ref[...], loads[0], NT)
        for s, out in enumerate(outs[1:]):
            out[: comps * kyb, :] = back[:, s * 2 * xb : (s + 1) * 2 * xb]
            if side is not None:
                out[comps * kyb :, :] = jnp.zeros((8, 2 * xb), F32)
                out[comps * kyb :, :kyb] = halo[8 * s : 8 * s + 8]

    one = (comps, 2, kyb, nx)
    spec_shape = (STEPS,) + one if step == STEPS - 1 else one
    height = comps * kyb + (0 if side is None else 8)
    outs = [(spec_shape, F32)] + [((height, 2 * xb), F32)] * rows
    args = ([] if side is None else [side]) + [*blocks, *table, past, kernel, *before]
    spec, *pieces = call(body, outs, *args)
    return spec, pieces


def turn(blocks, dims, comps, after):
    rows, _, xb, _, kyb = dims
    main, wide = comps * xb, 2 * rows * kyb
    sides = blocks[0].shape[0] > comps * kyb

    def body(*refs):
        *blocks, out = refs
        for comp in range(comps):
            line = slice(comp * kyb, (comp + 1) * kyb)
            flat = jnp.concatenate([ref[line, :] for ref in blocks], axis=0).T
            out[comp * xb : (comp + 1) * xb, :] = jnp.concatenate([flat[:xb], flat[xb:]], axis=1)
        if sides:
            low = comps * kyb
            parts = [ref[low + 4 * p : low + 4 * p + 4, :kyb] for p in range(2) for ref in blocks]
            out[main : main + 8, :] = jnp.zeros((8, wide), F32)
            out[main : main + 4, :] = jnp.concatenate(parts, axis=1)

    return call(body, [((main + (8 if sides else 0), wide), F32)], *blocks, after=after)[0]


def y_inverse(d_ref, hi, lo, dims, side_ref):
    xb, yb, depth = dims[2], dims[3], dims[1] // 2
    total = dot3(split(d_ref[...]), (hi[...], lo[...]), NN)
    if side_ref is None:
        return total
    beside = dot6(side_ref[...], d_ref[xb : 2 * xb, :], NT)
    gap = jnp.zeros((8, yb - xb), F32)
    parts = [jnp.concatenate([beside[8 * t : 8 * t + 8], gap], axis=1) for t in range(depth)]
    return jnp.concatenate([total, jnp.concatenate(parts, axis=1)], axis=0)


def part_inverse(data, table, dims, side=None):
    def body(d_ref, hi, lo, *refs):
        out = refs[-1]
        out[...] = y_inverse(d_ref, hi, lo, dims, refs[0] if side is not None else None)

    shape = (data.shape[0] + (0 if side is None else 8), dims[1] // 2 * dims[3])
    extra = [] if side is None else [side]
    return call(body, [(shape, F32)], data, *table, *extra)[0]


def rest_inverse(mine, data, table, dims, side=None):
    cols, yb = dims[1], dims[3]

    def body(m_ref, d_ref, hi, lo, *refs):
        side_ref, outs = (None, refs) if side is None else (refs[0], refs[1:])
        total = m_ref[...] + y_inverse(d_ref, hi, lo, dims, side_ref)
        for t, out in enumerate(outs):
            out[...] = total[:, t * yb : (t + 1) * yb]

    outs = [((mine.shape[0], yb), F32)] * (cols // 2)
    extra = [] if side is None else [side]
    return call(body, outs, mine, data, *table, *extra)


def in_turn(blocks):
    moved = []
    for t, block in enumerate(blocks, 1):
        moved.append(depth_perm(block, t))
    return moved


def gather_depth(block):
    return [block] + in_turn([block] * (lax.axis_size("col") // 2 - 1))


def forward(faces, borders, tables_, dims, after):
    mine, other = tables_[:2]
    edge, first, last = borders
    sent = part_forward(faces, other, dims, after=(first, *after))
    came = partner_perm(sent)
    kept = part_forward(faces, mine, dims)
    pieces = join(kept, came, first, last, dims)
    pieces = pieces[:1] + [shift_perm(pieces[s], "row", s) for s in range(1, dims[0])]
    beside = exchange_edges(edge)
    return pieces, (pieces[1], pieces[-1], *beside)


def inverse(pieces, tables_, dims, comps, last, after):
    mine, other, _, (side_mine, side_other, _) = tables_
    rows, _ = dims[:2]
    pieces = pieces[:1] + [shift_perm(pieces[s], "row", -s) for s in range(1, rows)]
    flat = turn(pieces, dims, comps, after)
    flat_other = partner_perm(flat)
    total = part_inverse(flat, mine, dims, None if last else side_mine)
    pieces = rest_inverse(total, flat_other, other, dims, None if last else side_other)
    return pieces[:1] + in_turn(pieces[1:])


def on_device(velocity, stress, buoyancy, lame, shear, kernel, history):
    rows, cols = lax.axis_size("row"), lax.axis_size("col")
    xb, yb = velocity.shape[2:]
    kyb = kernel.shape[3]
    dims = (rows, cols, xb, yb, kyb)
    where = jnp.stack([lax.axis_index("row"), lax.axis_index("col")]).astype(jnp.int32)

    halo = exchange(first_borders(stress))
    inner = inner_force(stress, velocity.shape[0])
    top = push_top(velocity, inner, buoyancy, halo)
    faces = gather_depth(top)
    tables_ = tables(where, dims)
    past = past_sums(kernel, history)
    recent = kernel[:STEPS]
    velocity, borders = push_rest(velocity, inner, buoyancy, halo, top)
    spectra = []
    traction = None
    for step in range(STEPS):
        last = step == STEPS - 1
        pieces, halo = forward(faces, borders, tables_, dims, () if last else past)
        side = None if last else tables_[3][2]
        spec, pieces = convolve(
            pieces, tables_[2], past[step], recent, spectra, dims, side
        )
        spectra.append(spec)
        stress, next_borders = push_stress(stress, velocity, lame, shear, halo, traction)
        after = () if last else (next_borders[1],)
        if not last:
            halo = exchange(next_borders)
        pieces = inverse(pieces, tables_, dims, recent.shape[1], last, after)
        if last:
            break
        velocity = push_velocity(velocity, stress, buoyancy, halo)
        traction, top = top_after(pieces, velocity, buoyancy)
        faces = gather_depth(top)
        velocity, borders = finish_velocity(velocity, buoyancy, traction, top)
    stress = add_traction(stress, pieces)
    return (velocity, stress, spectra[-1])


def solution(mesh):
    return jax.shard_map(
        on_device,
        mesh=mesh,
        in_specs=(
            P(None, None, "row", "col"),
            P(None, None, "row", "col"),
            P(None, "row", "col"),
            P(None, "row", "col"),
            P(None, "row", "col"),
            P(None, None, None, ("row", "col"), None),
            P(None, None, None, ("row", "col"), None),
        ),
        out_specs=(
            P(None, None, "row", "col"),
            P(None, None, "row", "col"),
            P(None, None, None, ("row", "col"), None),
        ),
        check_vma=False,
    )
```

```python
import math

import jax
import jax.numpy as jnp
from jax import lax
from jax.experimental import pallas as pl
from jax.experimental.pallas import tpu as pltpu
from jax.sharding import PartitionSpec as P


STEPS = 2
VMEM_LIMIT = 16 * 1024 * 1024
NEAR = 2.0 / 3.0
FAR = -1.0 / 12.0
F32 = jnp.float32
BF16 = jnp.bfloat16
NN = (((1,), (0,)), ((), ()))
NT = (((1,), (1,)), ((), ()))


def call(body, outs, *args, scratch=(), after=()):
    nbytes = sum(a.size * a.dtype.itemsize for a in args) + sum(
        math.prod(s) * jnp.dtype(d).itemsize for s, d in outs
    )
    count = len(args)

    def run(*refs):
        body(*refs[:count], *refs[count + len(after) :])

    results = pl.pallas_call(
        run,
        out_shape=[jax.ShapeDtypeStruct(s, d) for s, d in outs],
        in_specs=[
            pl.BlockSpec(memory_space=pltpu.SMEM if a.dtype == jnp.int32 else pltpu.VMEM)
            for a in args
        ]
        + [pl.BlockSpec(memory_space=pl.ANY) for _ in after],
        out_specs=[pl.BlockSpec(memory_space=pltpu.VMEM) for _ in outs],
        scratch_shapes=list(scratch),
        compiler_params=pltpu.CompilerParams(vmem_limit_bytes=VMEM_LIMIT),
        cost_estimate=pl.CostEstimate(flops=0, bytes_accessed=nbytes, transcendentals=0),
    )(*args, *after)
    return list(results)


def split(x):
    hi = x.astype(BF16)
    return hi, (x - hi.astype(F32)).astype(BF16)


def dot3(a, b, dims):
    a_hi, a_lo = a
    b_hi, b_lo = b

    def one(u, v):
        return lax.dot_general(u, v, dims, preferred_element_type=F32)

    return one(a_hi, b_hi) + (one(a_lo, b_hi) + one(a_hi, b_lo))


def dot6(a, b, dims):
    return lax.dot_general(
        a, b, dims, precision=lax.Precision.HIGHEST, preferred_element_type=F32
    )


def iota(shape, dim):
    return lax.broadcasted_iota(jnp.int32, shape, dim)


def shift_perm(x, axis, shift):
    count = lax.axis_size(axis)
    return lax.ppermute(x, axis, [(i, (i + shift) % count) for i in range(count)])


def depth_mask(t, odd, depth):
    return (depth - t) & (depth - 1) if odd else t


def depth_perm(x, t):
    count = lax.axis_size("col")
    return lax.ppermute(
        x, "col", [(i, i ^ (2 * depth_mask(t, i & 1, count // 2))) for i in range(count)]
    )


def partner_perm(x):
    count = lax.axis_size("col")
    return lax.ppermute(x, "col", [(i, i ^ 1) for i in range(count)])


def beyond(index, length):
    return jnp.where(index < 2, index - 2, index - 2 + length)


def tables(where, dims):
    rows, cols, xb, yb, kyb = dims
    nx, ny = rows * xb, cols * yb
    depth = cols // 2
    nk = rows * kyb

    def unit(phase, modulus):
        angle = (phase & (modulus - 1)).astype(F32) * (2.0 * math.pi / modulus)
        return jnp.cos(angle), jnp.sin(angle)

    def body(where_ref, oh, ol, ph, pl_, wh, wl, eo, ep, we):
        r, c = where_ref[0], where_ref[1]

        def met(t):
            turned = jnp.where((c & 1) == 1, (depth - t) & (depth - 1), t & (depth - 1))
            return c ^ (2 * turned)

        def put(hi_ref, lo_ref, index, value):
            hi, lo = split(value)
            hi_ref[index] = hi
            lo_ref[index] = lo

        line = iota((nk, yb), 0)
        lane = iota((nk, yb), 1)
        first_wave = ((line // kyb + r) & (rows - 1)) * (cols * kyb) + c * kyb + line % kyb
        own_cos, own_sin = unit(first_wave * lane, ny)
        hop = ((c ^ 1) - c) * kyb
        hop_cos, hop_sin = unit(hop * iota((8, yb), 1), ny)
        hop_cos, hop_sin = hop_cos[0:1], hop_sin[0:1]
        for flip, hi_ref, lo_ref, side_ref in ((0, oh, ol, eo), (1, ph, pl_, ep)):
            col = c ^ 1 if flip else c
            base_cos, base_sin = own_cos, own_sin
            if flip:
                base_cos = own_cos * hop_cos - own_sin * hop_sin
                base_sin = own_sin * hop_cos + own_cos * hop_sin
            turn = iota((max(8, depth), nk), 0)
            across = iota((max(8, depth), nk), 1)
            wave = ((across // kyb + r) & (rows - 1)) * (cols * kyb) + col * kyb + across % kyb
            turn_cos, turn_sin = unit(wave * ((met(turn)) * yb), ny)
            turn_cos, turn_sin = turn_cos.T, turn_sin.T
            scale = 1.0 / math.sqrt(ny)
            for t in range(depth):
                tc, ts = turn_cos[:, t : t + 1] * scale, turn_sin[:, t : t + 1] * scale
                span = pl.ds(t * yb, yb)
                put(hi_ref, lo_ref, (pl.ds(0, nk), span), base_cos * tc - base_sin * ts)
                put(hi_ref, lo_ref, (pl.ds(nk, nk), span), -(base_sin * tc + base_cos * ts))
            line, lane = iota((depth * 8, nk), 0), iota((depth * 8, nk), 1)
            wave = ((lane // kyb + r) & (rows - 1)) * (cols * kyb) + col * kyb + lane % kyb
            spot = (met(line // 8)) * yb + beyond(line % 8, yb)
            side_cos, side_sin = unit(wave * spot, ny)
            side_ref[:, :nk] = side_cos * scale
            side_ref[:, nk:] = -side_sin * scale
        base_cos, base_sin = unit(iota((xb, nx), 0) * iota((xb, nx), 1), nx)
        tall = max(8, rows)
        start = ((r - iota((tall, nx), 0)) & (rows - 1)) * xb
        turn_cos, turn_sin = unit(start * iota((tall, nx), 1), nx)
        scale = 1.0 / math.sqrt(nx)
        for s in range(rows):
            tc, ts = turn_cos[s : s + 1] * scale, turn_sin[s : s + 1] * scale
            cos = base_cos * tc - base_sin * ts
            sin = base_sin * tc + base_cos * ts
            top, low = pl.ds(2 * s * xb, xb), pl.ds((2 * s + 1) * xb, xb)
            put(wh, wl, (top, pl.ds(0, nx)), cos)
            put(wh, wl, (top, pl.ds(nx, nx)), -sin)
            put(wh, wl, (low, pl.ds(0, nx)), sin)
            put(wh, wl, (low, pl.ds(nx, nx)), cos)
        line, lane = iota((rows * 8, nx), 0), iota((rows * 8, nx), 1)
        spot = ((r - line // 8) & (rows - 1)) * xb + beyond(line % 4, xb)
        cos, sin = unit(spot * lane, nx)
        real = line % 8 < 4
        we[:, :nx] = jnp.where(real, cos, sin) * scale
        we[:, nx:] = jnp.where(real, -sin, cos) * scale

    y_shape, x_shape = (2 * nk, depth * yb), (2 * nx, 2 * nx)
    outs = [(y_shape, BF16)] * 4 + [(x_shape, BF16)] * 2
    outs += [((depth * 8, 2 * nk), F32)] * 2 + [((rows * 8, 2 * nx), F32)]
    oh, ol, ph, pl_, wh, wl, eo, ep, we = call(body, outs, where)
    return (oh, ol), (ph, pl_), (wh, wl), (eo, ep, we)


def past_sums(kernel, history):
    lags, comps, _, kyb, nx = kernel.shape

    def body(k_ref, h_ref, *out_refs):
        for comp in range(comps):
            line = pl.ds(comp * kyb, kyb)
            totals = [[None, None] for _ in range(STEPS)]
            for lag in range(1, lags):
                kr = k_ref[lag, comp, 0].astype(F32)
                ki = k_ref[lag, comp, 1].astype(F32)
                for step in range(STEPS):
                    if lag - 1 < step:
                        continue
                    hr = h_ref[lag - 1 - step, comp, 0].astype(F32)
                    hi = h_ref[lag - 1 - step, comp, 1].astype(F32)
                    for part, value in enumerate((kr * hr - ki * hi, kr * hi + ki * hr)):
                        old = totals[step][part]
                        totals[step][part] = value if old is None else old + value
            for step in range(STEPS):
                for part in range(2):
                    out_refs[step][line, pl.ds(part * nx, nx)] = totals[step][part]

    return call(body, [((comps * kyb, 2 * nx), F32)] * STEPS, kernel, history)


ROW_PARTS = (0, 3, 4)
COL_PARTS = (3, 1, 5)


def edge_weights(yb):
    line, lane = iota((8, yb), 0), iota((8, yb), 1)
    target = jnp.where(line < 2, line, yb - 4 + line)
    return jnp.where((lane == target) & (line < 4), 1.0, 0.0).astype(F32)


def inner_weights(yb):
    gap = iota((yb, yb), 0) - iota((yb, yb), 1)
    value = jnp.where(gap == 1, NEAR, 0.0) - jnp.where(gap == -1, NEAR, 0.0)
    return value + jnp.where(gap == 2, FAR, 0.0) - jnp.where(gap == -2, FAR, 0.0)


def outer_weights(yb, where_ref):
    line, lane = iota((8, yb), 0), iota((8, yb), 1)
    left_gap = jnp.where((line == 2) | (line == 3), line - 4 - lane, 99)
    right_gap = jnp.where(line < 2, yb + line - lane, 99)

    def value(gap):
        near = jnp.where(gap == 1, NEAR, 0.0) - jnp.where(gap == -1, NEAR, 0.0)
        return near + jnp.where(gap == 2, FAR, 0.0) - jnp.where(gap == -2, FAR, 0.0)

    left, right = value(left_gap), value(right_gap)
    odd = (where_ref[1] & 1) == 1
    return jnp.where(odd, left, right), jnp.where(odd, right, left)


def put_borders(planes, row_planes, col_planes, edge_ref, first_ref, last_ref):
    xb, yb = planes(row_planes[0]).shape
    for j, which in enumerate(row_planes):
        plane = planes(which)
        first_ref[2 * j : 2 * j + 2, :] = plane[:2]
        last_ref[2 * j : 2 * j + 2, :] = plane[xb - 2 :]
    stacked = jnp.concatenate([planes(which) for which in col_planes], axis=0)
    edge_ref[...] = dot6(edge_weights(yb), stacked, NT)


def row_deriv(pad_ref, plane, above, below):
    xb = plane.shape[0]
    pad_ref[8 : 8 + xb, :] = plane
    pad_ref[6:8, :] = above
    pad_ref[8 + xb : 10 + xb, :] = below
    near = pad_ref[9 : 9 + xb, :] - pad_ref[7 : 7 + xb, :]
    far = pad_ref[10 : 10 + xb, :] - pad_ref[6 : 6 + xb, :]
    return NEAR * near + FAR * far


def col_deriv(stacked, partner, across, partner_w, across_w):
    yb = stacked.shape[1]
    inner = dot6(stacked, inner_weights(yb), NN)
    return inner + (dot6(partner.T, partner_w, NN) + dot6(across.T, across_w, NN))


def depth_deriv(at, layer, layers):
    total = None
    for step, weight in ((1, NEAR), (-1, -NEAR), (2, FAR), (-2, -FAR)):
        if 0 <= layer + step < layers:
            term = weight * at(layer + step)
            total = term if total is None else total + term
    return total


def borders_shapes(layers, xb, yb):
    planes = 3 * layers
    return [((8, planes * xb), F32), ((2 * planes, yb), F32), ((2 * planes, yb), F32)]


def row_patch(above, below, xb):
    line, lane = iota((xb, 4), 0), iota((xb, 4), 1)
    gap = beyond(lane, xb) - line
    near = jnp.where(gap == 1, NEAR, 0.0) - jnp.where(gap == -1, NEAR, 0.0)
    weights = near + jnp.where(gap == 2, FAR, 0.0) - jnp.where(gap == -2, FAR, 0.0)
    total = weights[:, 0:1] * above[0:1] + weights[:, 1:2] * above[1:2]
    return total + (weights[:, 2:3] * below[0:1] + weights[:, 3:4] * below[1:2])


def plane_list(parts, layers):
    return [(p, l) for p in parts for l in range(layers)]


def first_borders(stress):
    _, layers, xb, yb = stress.shape

    def body(s_ref, *outs):
        rows, cols = plane_list(ROW_PARTS, layers), plane_list(COL_PARTS, layers)
        put_borders(lambda w: s_ref[w[0], w[1]], rows, cols, *outs)

    return call(body, borders_shapes(layers, xb, yb), stress)


def exchange_edges(edge):
    count = lax.axis_size("col")
    across = [(i, (i + 1 if i & 1 else i - 1) % count) for i in range(count)]
    return partner_perm(edge), lax.ppermute(edge, "col", across)


def exchange(borders):
    edge, first, last = borders
    above = shift_perm(last, "row", 1)
    below = shift_perm(first, "row", -1)
    return (above, below, *exchange_edges(edge))


DEPTH_PARTS = (4, 5, 2)


def inner_force(stress, comps):
    _, layers, xb, yb = stress.shape

    def body(s_ref, f_ref, pad):
        none = jnp.zeros((2, yb), F32)
        stacked = jnp.concatenate(
            [s_ref[p, l] for p, l in plane_list(COL_PARTS, layers)], axis=0
        )
        along_y = dot6(stacked, inner_weights(yb), NN)
        for comp in range(comps):
            for layer in range(layers):
                j = comp * layers + layer
                force = row_deriv(pad.at[j], s_ref[ROW_PARTS[comp], layer], none, none)
                force = force + along_y[j * xb : (j + 1) * xb]
                force = force + depth_deriv(lambda l: s_ref[DEPTH_PARTS[comp], l], layer, layers)
                f_ref[comp, layer] = force

    return call(
        body, [((comps, layers, xb, yb), F32)], stress,
        scratch=[pltpu.VMEM((comps * layers, xb + 16, yb), F32)],
    )[0]


def push_top(velocity, inner, buoyancy, halo):
    comps, layers, xb, yb = inner.shape

    def body(v_ref, f_ref, b_ref, up, dn, lf, rt, lw, rw, top_ref):
        left_w, right_w = lw[...], rw[...]
        for comp in range(comps):
            j = comp * layers
            pair, lane = slice(2 * j, 2 * j + 2), slice(j * xb, (j + 1) * xb)
            patch = row_patch(up[pair, :], dn[pair, :], xb)
            patch = patch + dot6(lf[:, lane].T, left_w, NN) + dot6(rt[:, lane].T, right_w, NN)
            push = b_ref[0] * (f_ref[comp, 0] + patch)
            top_ref[comp * xb : (comp + 1) * xb, :] = v_ref[comp, 0] + push

    return call(body, [((comps * xb, yb), F32)], velocity, inner, buoyancy, *halo)[0]


def push_rest(velocity, inner, buoyancy, halo, top):
    comps, layers, xb, yb = inner.shape

    def body(v_ref, f_ref, b_ref, up, dn, lf, rt, lw, rw, top_ref, nv_ref, edge, first, last):
        left_w, right_w = lw[...], rw[...]
        along_y = dot6(lf[...].T, left_w, NN) + dot6(rt[...].T, right_w, NN)
        for comp in range(comps):
            nv_ref[comp, 0] = top_ref[comp * xb : (comp + 1) * xb, :]
            for layer in range(1, layers):
                j = comp * layers + layer
                pair = slice(2 * j, 2 * j + 2)
                patch = row_patch(up[pair, :], dn[pair, :], xb) + along_y[j * xb : (j + 1) * xb]
                push = b_ref[layer] * (f_ref[comp, layer] + patch)
                nv_ref[comp, layer] = v_ref[comp, layer] + push
        planes = plane_list(range(comps), layers)
        put_borders(lambda w: nv_ref[w[0], w[1]], planes, planes, edge, first, last)

    outs = [(inner.shape, F32)] + borders_shapes(layers, xb, yb)
    new, *borders = call(body, outs, velocity, inner, buoyancy, *halo, top)
    return new, borders


def push_velocity(velocity, stress, buoyancy, halo):
    comps, layers, xb, yb = velocity.shape

    def body(v_ref, s_ref, b_ref, up, dn, lf, rt, lw, rw, nv_ref, pad):
        stacked = jnp.concatenate(
            [s_ref[p, l] for p, l in plane_list(COL_PARTS, layers)], axis=0
        )
        along_y = col_deriv(stacked, lf[...], rt[...], lw[...], rw[...])
        for comp in range(comps):
            for layer in range(layers):
                j = comp * layers + layer
                pair = slice(2 * j, 2 * j + 2)
                force = row_deriv(pad.at[j], s_ref[ROW_PARTS[comp], layer], up[pair, :], dn[pair, :])
                force = force + along_y[j * xb : (j + 1) * xb]
                force = force + depth_deriv(lambda l: s_ref[DEPTH_PARTS[comp], l], layer, layers)
                nv_ref[comp, layer] = v_ref[comp, layer] + b_ref[layer] * force

    return call(
        body, [(velocity.shape, F32)], velocity, stress, buoyancy, *halo,
        scratch=[pltpu.VMEM((comps * layers, xb + 16, yb), F32)],
    )[0]


def push_stress(stress, velocity, lame, shear, halo, traction=None):
    comps, layers, xb, yb = velocity.shape

    def body(s_ref, v_ref, l_ref, m_ref, up, dn, lf, rt, lw, rw, *refs):
        stacked = jnp.concatenate(
            [v_ref[c, l] for c, l in plane_list(range(comps), layers)], axis=0
        )
        if traction is None:
            ns_ref, *outs, pad = refs
        else:
            t_ref, ns_ref, face_ref, pad = refs
        along_y = col_deriv(stacked, lf[...], rt[...], lw[...], rw[...])
        skip = up.shape[0] - 2 * comps * layers
        for layer in range(layers):
            gx, gy, gz = [], [], []
            for comp in range(comps):
                j = comp * layers + layer
                pair = slice(skip + 2 * j, skip + 2 * j + 2)
                gx.append(row_deriv(pad.at[j], v_ref[comp, layer], up[pair, :], dn[pair, :]))
                gy.append(along_y[j * xb : (j + 1) * xb])
                gz.append(depth_deriv(lambda l: v_ref[comp, l], layer, layers))
            lam, mu = l_ref[layer], m_ref[layer]
            spread = lam * (gx[0] + gy[1] + gz[2])
            twice = 2.0 * mu
            old = [s_ref[part, layer] for part in range(6)]
            if traction is not None and layer == 0:
                for comp, part in enumerate(DEPTH_PARTS):
                    old[part] = old[part] + t_ref[comp * xb : (comp + 1) * xb, :]
            ns_ref[0, layer] = old[0] + spread + twice * gx[0]
            ns_ref[1, layer] = old[1] + spread + twice * gy[1]
            ns_ref[2, layer] = old[2] + spread + twice * gz[2]
            ns_ref[3, layer] = old[3] + mu * (gy[0] + gx[1])
            ns_ref[4, layer] = old[4] + mu * (gz[0] + gx[2])
            ns_ref[5, layer] = old[5] + mu * (gz[1] + gy[2])
        if traction is None:
            rows, cols = plane_list(ROW_PARTS, layers), plane_list(COL_PARTS, layers)
            put_borders(lambda w: ns_ref[w[0], w[1]], rows, cols, *outs)
        else:
            for comp, part in enumerate(DEPTH_PARTS):
                face_ref[comp * xb : (comp + 1) * xb, :] = ns_ref[part, 0]

    args = [stress, velocity, lame, shear, *halo] + ([] if traction is None else [traction])
    outs = [(stress.shape, F32)]
    outs += borders_shapes(layers, xb, yb) if traction is None else [((comps * xb, yb), F32)]
    new, *borders = call(
        body, outs, *args,
        scratch=[pltpu.VMEM((comps * layers, xb + 16, yb), F32)],
    )
    return new, borders


def total_of(refs):
    total = refs[0][...]
    for ref in refs[1:]:
        total = total + ref[...]
    return total


def top_after(pieces, velocity, buoyancy):
    comps, _, xb, yb = velocity.shape
    height = pieces[0].shape[0]

    def body(v_ref, b_ref, *refs):
        *piece_refs, sum_ref, face_ref, pad = refs
        total = total_of(piece_refs)
        sum_ref[...] = total
        main = comps * xb
        force = row_deriv(pad, total[:xb], total[main : main + 2], total[main + 2 : main + 4])
        side = total[main + 8 : main + 16, :xb].T
        line, lane = iota((8, yb), 0), iota((8, yb), 1)
        gap = jnp.where(line < 4, beyond(line, yb) - lane, 99)
        near = jnp.where(gap == 1, NEAR, 0.0) - jnp.where(gap == -1, NEAR, 0.0)
        outer = near + jnp.where(gap == 2, FAR, 0.0) - jnp.where(gap == -2, FAR, 0.0)
        force = force + (dot6(total[xb : 2 * xb], inner_weights(yb), NN) + dot6(side, outer, NN))
        for comp in range(comps - 1):
            face_ref[comp * xb : (comp + 1) * xb, :] = v_ref[comp, 0]
        face_ref[(comps - 1) * xb :, :] = v_ref[comps - 1, 0] + b_ref[0] * force

    return call(
        body, [((height, yb), F32), ((comps * xb, yb), F32)], velocity, buoyancy, *pieces,
        scratch=[pltpu.VMEM((xb + 16, yb), F32)],
    )


def finish_velocity(velocity, buoyancy, traction, face):
    comps, layers, xb, yb = velocity.shape

    def body(v_ref, b_ref, t_ref, f_ref, nv_ref, edge, first, last):
        for comp in range(comps):
            push = t_ref[comp * xb : (comp + 1) * xb, :]
            for layer in range(layers):
                new = v_ref[comp, layer]
                if layer == 0 and comp == comps - 1:
                    new = f_ref[comp * xb :, :]
                if layer in (1, 2):
                    weight = -NEAR if layer == 1 else -FAR
                    new = new + b_ref[layer] * (weight * push)
                nv_ref[comp, layer] = new
        planes = plane_list(range(comps), layers)
        put_borders(lambda w: nv_ref[w[0], w[1]], planes, planes, edge, first, last)

    outs = [(velocity.shape, F32)] + borders_shapes(layers, xb, yb)
    new, *borders = call(body, outs, velocity, buoyancy, traction, face)
    return new, borders


def add_traction(stress, faces, pieces):
    xb, yb = stress.shape[2:]
    comps = len(DEPTH_PARTS)

    def body(s_ref, f_ref, *refs):
        *piece_refs, ns_ref, new_ref, sems = refs
        new_ref[...] = f_ref[...] + total_of(piece_refs)
        copies = [
            pltpu.make_async_copy(
                new_ref.at[pl.ds(comp * xb, xb)], ns_ref.at[part, 0], sems.at[comp]
            )
            for comp, part in enumerate(DEPTH_PARTS)
        ]
        for copy in copies:
            copy.start()
        for copy in copies:
            copy.wait()

    anywhere = pl.BlockSpec(memory_space=pl.ANY)
    inside = pl.BlockSpec(memory_space=pltpu.VMEM)
    return pl.pallas_call(
        body,
        name="traction",
        out_shape=jax.ShapeDtypeStruct(stress.shape, F32),
        in_specs=[anywhere] + [inside] * (1 + len(pieces)),
        out_specs=anywhere,
        scratch_shapes=[pltpu.VMEM((comps * xb, yb), F32), pltpu.SemaphoreType.DMA((comps,))],
        input_output_aliases={0: 0},
        compiler_params=pltpu.CompilerParams(vmem_limit_bytes=VMEM_LIMIT),
        cost_estimate=pl.CostEstimate(
            flops=0, bytes_accessed=8 * comps * xb * yb, transcendentals=0
        ),
    )(stress, faces, *pieces)


def part_forward(blocks, table, dims, after=()):
    rows, _, xb, _, kyb = dims
    nk = rows * kyb
    comps = blocks[0].shape[0] // xb

    def body(*refs):
        hi, lo, out = refs[-3:]
        data = jnp.concatenate([ref[...] for ref in refs[:-3]], axis=1)
        total = dot3((hi[...], lo[...]), split(data), NT)
        for s in range(rows):
            for comp in range(comps):
                lane = slice(comp * xb, (comp + 1) * xb)
                real = total[s * kyb : (s + 1) * kyb, lane]
                imag = total[nk + s * kyb : nk + (s + 1) * kyb, lane]
                at = (s * comps + comp) * kyb
                out[at : at + kyb, :] = jnp.concatenate([real, imag], axis=1)

    return call(body, [((rows * comps * kyb, 2 * xb), F32)], *blocks, *table, after=after)[0]


def join(mine, other, first, last, dims):
    rows = dims[0]
    height, extra = mine.shape[0] // rows, first.shape[0]
    riders = {1: 1, rows - 1: 0}

    def body(a_ref, b_ref, *refs):
        borders, outs = refs[:2], refs[2:]
        for s, out in enumerate(outs):
            span = slice(s * height, (s + 1) * height)
            out[:height, :] = a_ref[span, :] + b_ref[span, :]
            if s in riders:
                out[height:, :] = borders[riders[s]][...]

    outs = [((height + (extra if s in riders else 0), mine.shape[1]), F32) for s in range(rows)]
    return call(body, outs, mine, other, first, last)


def convolve(blocks, table, past, kernel, before, dims, side=None):
    rows, _, xb, _, kyb = dims
    nx = rows * xb
    comps = blocks[0].shape[0] // kyb
    step = len(before)

    def body(*refs):
        if side is not None:
            side_ref, *refs = refs
        ins, outs = refs[: rows + 4 + step], refs[rows + 4 + step :]
        wide = (ins[rows][...], ins[rows + 1][...])
        past_ref, k_ref, olds = ins[rows + 2], ins[rows + 3], ins[rows + 4 :]
        data = jnp.concatenate([ref[: comps * kyb, :] for ref in ins[:rows]], axis=1)
        spec = dot3(split(data), wide, NN)
        spec_ref = outs[0]
        loads = []
        for comp in range(comps):
            line = slice(comp * kyb, (comp + 1) * kyb)
            now = (spec[line, :nx], spec[line, nx:])
            spec_ref[comp, 0] = now[0]
            spec_ref[comp, 1] = now[1]
            real, imag = past_ref[line, :nx], past_ref[line, nx:]
            terms = [now] + [(old[comp, 0], old[comp, 1]) for old in reversed(olds)]
            for lag, (sr, si) in enumerate(terms):
                kr, ki = k_ref[lag, comp, 0].astype(F32), k_ref[lag, comp, 1].astype(F32)
                real = real + (kr * sr - ki * si)
                imag = imag + (kr * si + ki * sr)
            loads.append(jnp.concatenate([real, imag], axis=1))
        back = dot3(split(jnp.concatenate(loads, axis=0)), wide, NT)
        if side is not None:
            halo = dot6(side_ref[...], loads[0], NT)
        for s, out in enumerate(outs[1:]):
            out[: comps * kyb, :] = back[:, s * 2 * xb : (s + 1) * 2 * xb]
            if side is not None:
                out[comps * kyb :, :] = jnp.zeros((8, 2 * xb), F32)
                out[comps * kyb :, :kyb] = halo[8 * s : 8 * s + 8]

    spec_shape = (comps, 2, kyb, nx)
    height = comps * kyb + (0 if side is None else 8)
    outs = [(spec_shape, F32)] + [((height, 2 * xb), F32)] * rows
    args = ([] if side is None else [side]) + [*blocks, *table, past, kernel, *before]
    spec, *pieces = call(body, outs, *args)
    return spec, pieces


def collect(spectra):
    def body(*refs):
        *ins, out = refs
        for n, ref in enumerate(ins):
            out[n] = ref[...]

    return call(body, [((len(spectra),) + spectra[0].shape, F32)], *spectra)[0]


def turn(blocks, dims, comps, after):
    rows, _, xb, _, kyb = dims
    main, wide = comps * xb, 2 * rows * kyb
    sides = blocks[0].shape[0] > comps * kyb

    def body(*refs):
        *blocks, out = refs
        for comp in range(comps):
            line = slice(comp * kyb, (comp + 1) * kyb)
            flat = jnp.concatenate([ref[line, :] for ref in blocks], axis=0).T
            out[comp * xb : (comp + 1) * xb, :] = jnp.concatenate([flat[:xb], flat[xb:]], axis=1)
        if sides:
            low = comps * kyb
            parts = [ref[low + 4 * p : low + 4 * p + 4, :kyb] for p in range(2) for ref in blocks]
            out[main : main + 8, :] = jnp.zeros((8, wide), F32)
            out[main : main + 4, :] = jnp.concatenate(parts, axis=1)

    return call(body, [((main + (8 if sides else 0), wide), F32)], *blocks, after=after)[0]


def y_inverse(d_ref, hi, lo, dims, side_ref):
    xb, yb, depth = dims[2], dims[3], dims[1] // 2
    total = dot3(split(d_ref[...]), (hi[...], lo[...]), NN)
    if side_ref is None:
        return total
    beside = dot6(side_ref[...], d_ref[xb : 2 * xb, :], NT)
    gap = jnp.zeros((8, yb - xb), F32)
    parts = [jnp.concatenate([beside[8 * t : 8 * t + 8], gap], axis=1) for t in range(depth)]
    return jnp.concatenate([total, jnp.concatenate(parts, axis=1)], axis=0)


def part_inverse(data, table, dims, side=None):
    def body(d_ref, hi, lo, *refs):
        out = refs[-1]
        out[...] = y_inverse(d_ref, hi, lo, dims, refs[0] if side is not None else None)

    shape = (data.shape[0] + (0 if side is None else 8), dims[1] // 2 * dims[3])
    extra = [] if side is None else [side]
    return call(body, [(shape, F32)], data, *table, *extra)[0]


def rest_inverse(mine, data, table, dims, side=None):
    cols, yb = dims[1], dims[3]

    def body(m_ref, d_ref, hi, lo, *refs):
        side_ref, outs = (None, refs) if side is None else (refs[0], refs[1:])
        total = m_ref[...] + y_inverse(d_ref, hi, lo, dims, side_ref)
        for t, out in enumerate(outs):
            out[...] = total[:, t * yb : (t + 1) * yb]

    outs = [((mine.shape[0], yb), F32)] * (cols // 2)
    extra = [] if side is None else [side]
    return call(body, outs, mine, data, *table, *extra)


def in_turn(blocks):
    moved = []
    for t, block in enumerate(blocks, 1):
        moved.append(depth_perm(block, t))
    return moved


def gather_depth(block):
    return [block] + in_turn([block] * (lax.axis_size("col") // 2 - 1))


def forward(faces, borders, tables_, dims, after):
    mine, other = tables_[:2]
    edge, first, last = borders
    sent = part_forward(faces, other, dims, after=(first, *after))
    came = partner_perm(sent)
    kept = part_forward(faces, mine, dims)
    pieces = join(kept, came, first, last, dims)
    pieces = pieces[:1] + [shift_perm(pieces[s], "row", s) for s in range(1, dims[0])]
    beside = exchange_edges(edge)
    return pieces, (pieces[1], pieces[-1], *beside)


def inverse(pieces, tables_, dims, comps, last, after):
    mine, other, _, (side_mine, side_other, _) = tables_
    rows, _ = dims[:2]
    pieces = pieces[:1] + [shift_perm(pieces[s], "row", -s) for s in range(1, rows)]
    flat = turn(pieces, dims, comps, after)
    flat_other = partner_perm(flat)
    total = part_inverse(flat, mine, dims, None if last else side_mine)
    pieces = rest_inverse(total, flat_other, other, dims, None if last else side_other)
    return pieces[:1] + in_turn(pieces[1:])


def on_device(velocity, stress, buoyancy, lame, shear, kernel, history):
    rows, cols = lax.axis_size("row"), lax.axis_size("col")
    xb, yb = velocity.shape[2:]
    kyb = kernel.shape[3]
    dims = (rows, cols, xb, yb, kyb)
    where = jnp.stack([lax.axis_index("row"), lax.axis_index("col")]).astype(jnp.int32)

    halo = exchange(first_borders(stress))
    inner = inner_force(stress, velocity.shape[0])
    weights = outer_weights(yb, where)
    halo = (*halo, *weights)
    top = push_top(velocity, inner, buoyancy, halo)
    faces = gather_depth(top)
    tables_ = tables(where, dims)
    past = past_sums(kernel, history)
    recent = kernel[:STEPS]
    velocity, borders = push_rest(velocity, inner, buoyancy, halo, top)
    spectra = []
    traction = None
    for step in range(STEPS):
        last = step == STEPS - 1
        pieces, halo = forward(faces, borders, tables_, dims, () if last else past)
        halo = (*halo, *weights)
        side = None if last else tables_[3][2]
        spec, pieces = convolve(
            pieces, tables_[2], past[step], recent, spectra, dims, side
        )
        spectra.append(spec)
        stress, next_borders = push_stress(stress, velocity, lame, shear, halo, traction)
        after = () if last else (next_borders[1],)
        if not last:
            halo = (*exchange(next_borders), *weights)
        pieces = inverse(pieces, tables_, dims, recent.shape[1], last, after)
        if last:
            break
        velocity = push_velocity(velocity, stress, buoyancy, halo)
        traction, top = top_after(pieces, velocity, buoyancy)
        faces = gather_depth(top)
        velocity, borders = finish_velocity(velocity, buoyancy, traction, top)
    spectra = collect(spectra)
    stress = add_traction(stress, *next_borders, pieces)
    return (velocity, stress, spectra)


def solution(mesh):
    return jax.shard_map(
        on_device,
        mesh=mesh,
        in_specs=(
            P(None, None, "row", "col"),
            P(None, None, "row", "col"),
            P(None, "row", "col"),
            P(None, "row", "col"),
            P(None, "row", "col"),
            P(None, None, None, ("row", "col"), None),
            P(None, None, None, ("row", "col"), None),
        ),
        out_specs=(
            P(None, None, "row", "col"),
            P(None, None, "row", "col"),
            P(None, None, None, ("row", "col"), None),
        ),
        check_vma=False,
    )
```

```python
import math

import jax
import jax.numpy as jnp
from jax import lax
from jax.experimental import pallas as pl
from jax.experimental.pallas import tpu as pltpu
from jax.sharding import PartitionSpec as P


STEPS = 2
VMEM_LIMIT = 16 * 1024 * 1024
NEAR = 2.0 / 3.0
FAR = -1.0 / 12.0
F32 = jnp.float32
BF16 = jnp.bfloat16
NN = (((1,), (0,)), ((), ()))
NT = (((1,), (1,)), ((), ()))


def call(body, outs, *args, scratch=(), after=()):
    nbytes = sum(a.size * a.dtype.itemsize for a in args) + sum(
        math.prod(s) * jnp.dtype(d).itemsize for s, d in outs
    )
    count = len(args)

    def run(*refs):
        body(*refs[:count], *refs[count + len(after) :])

    results = pl.pallas_call(
        run,
        out_shape=[jax.ShapeDtypeStruct(s, d) for s, d in outs],
        in_specs=[
            pl.BlockSpec(memory_space=pltpu.SMEM if a.dtype == jnp.int32 else pltpu.VMEM)
            for a in args
        ]
        + [pl.BlockSpec(memory_space=pl.ANY) for _ in after],
        out_specs=[pl.BlockSpec(memory_space=pltpu.VMEM) for _ in outs],
        scratch_shapes=list(scratch),
        compiler_params=pltpu.CompilerParams(vmem_limit_bytes=VMEM_LIMIT),
        cost_estimate=pl.CostEstimate(flops=0, bytes_accessed=nbytes, transcendentals=0),
    )(*args, *after)
    return list(results)


def split(x):
    hi = x.astype(BF16)
    return hi, (x - hi.astype(F32)).astype(BF16)


def dot3(a, b, dims):
    a_hi, a_lo = a
    b_hi, b_lo = b

    def one(u, v):
        return lax.dot_general(u, v, dims, preferred_element_type=F32)

    return one(a_hi, b_hi) + (one(a_lo, b_hi) + one(a_hi, b_lo))


def dot6(a, b, dims):
    return lax.dot_general(
        a, b, dims, precision=lax.Precision.HIGHEST, preferred_element_type=F32
    )


def iota(shape, dim):
    return lax.broadcasted_iota(jnp.int32, shape, dim)


def shift_perm(x, axis, shift):
    count = lax.axis_size(axis)
    return lax.ppermute(x, axis, [(i, (i + shift) % count) for i in range(count)])


def depth_mask(t, odd, depth):
    return (depth - t) & (depth - 1) if odd else t


def depth_perm(x, t):
    count = lax.axis_size("col")
    return lax.ppermute(
        x, "col", [(i, i ^ (2 * depth_mask(t, i & 1, count // 2))) for i in range(count)]
    )


def partner_perm(x):
    count = lax.axis_size("col")
    return lax.ppermute(x, "col", [(i, i ^ 1) for i in range(count)])


def beyond(index, length):
    return jnp.where(index < 2, index - 2, index - 2 + length)


def tables(where, dims):
    rows, cols, xb, yb, kyb = dims
    nx, ny = rows * xb, cols * yb
    depth = cols // 2
    nk = rows * kyb

    def unit(phase, modulus):
        angle = (phase & (modulus - 1)).astype(F32) * (2.0 * math.pi / modulus)
        return jnp.cos(angle), jnp.sin(angle)

    def body(where_ref, oh, ol, ph, pl_, wh, wl, eo, ep, we):
        r, c = where_ref[0], where_ref[1]

        def met(t):
            turned = jnp.where((c & 1) == 1, (depth - t) & (depth - 1), t & (depth - 1))
            return c ^ (2 * turned)

        def put(hi_ref, lo_ref, index, value):
            hi, lo = split(value)
            hi_ref[index] = hi
            lo_ref[index] = lo

        line = iota((nk, yb), 0)
        lane = iota((nk, yb), 1)
        first_wave = ((line // kyb + r) & (rows - 1)) * (cols * kyb) + c * kyb + line % kyb
        own_cos, own_sin = unit(first_wave * lane, ny)
        hop = ((c ^ 1) - c) * kyb
        hop_cos, hop_sin = unit(hop * iota((8, yb), 1), ny)
        hop_cos, hop_sin = hop_cos[0:1], hop_sin[0:1]
        for flip, hi_ref, lo_ref, side_ref in ((0, oh, ol, eo), (1, ph, pl_, ep)):
            col = c ^ 1 if flip else c
            base_cos, base_sin = own_cos, own_sin
            if flip:
                base_cos = own_cos * hop_cos - own_sin * hop_sin
                base_sin = own_sin * hop_cos + own_cos * hop_sin
            turn = iota((max(8, depth), nk), 0)
            across = iota((max(8, depth), nk), 1)
            wave = ((across // kyb + r) & (rows - 1)) * (cols * kyb) + col * kyb + across % kyb
            turn_cos, turn_sin = unit(wave * ((met(turn)) * yb), ny)
            turn_cos, turn_sin = turn_cos.T, turn_sin.T
            scale = 1.0 / math.sqrt(ny)
            for t in range(depth):
                tc, ts = turn_cos[:, t : t + 1] * scale, turn_sin[:, t : t + 1] * scale
                span = pl.ds(t * yb, yb)
                put(hi_ref, lo_ref, (pl.ds(0, nk), span), base_cos * tc - base_sin * ts)
                put(hi_ref, lo_ref, (pl.ds(nk, nk), span), -(base_sin * tc + base_cos * ts))
            line, lane = iota((depth * 8, nk), 0), iota((depth * 8, nk), 1)
            wave = ((lane // kyb + r) & (rows - 1)) * (cols * kyb) + col * kyb + lane % kyb
            spot = (met(line // 8)) * yb + beyond(line % 8 - 4, yb)
            side_cos, side_sin = unit(wave * spot, ny)
            used = line % 8 >= 4
            side_ref[:, :nk] = jnp.where(used, side_cos * scale, 0.0)
            side_ref[:, nk:] = jnp.where(used, -side_sin * scale, 0.0)
        base_cos, base_sin = unit(iota((xb, nx), 0) * iota((xb, nx), 1), nx)
        tall = max(8, rows)
        start = ((r - iota((tall, nx), 0)) & (rows - 1)) * xb
        turn_cos, turn_sin = unit(start * iota((tall, nx), 1), nx)
        scale = 1.0 / math.sqrt(nx)
        for s in range(rows):
            tc, ts = turn_cos[s : s + 1] * scale, turn_sin[s : s + 1] * scale
            cos = base_cos * tc - base_sin * ts
            sin = base_sin * tc + base_cos * ts
            top, low = pl.ds(2 * s * xb, xb), pl.ds((2 * s + 1) * xb, xb)
            put(wh, wl, (top, pl.ds(0, nx)), cos)
            put(wh, wl, (top, pl.ds(nx, nx)), -sin)
            put(wh, wl, (low, pl.ds(0, nx)), sin)
            put(wh, wl, (low, pl.ds(nx, nx)), cos)
        line, lane = iota((rows * 8, nx), 0), iota((rows * 8, nx), 1)
        spot = ((r - line // 8) & (rows - 1)) * xb + beyond(line % 4, xb)
        cos, sin = unit(spot * lane, nx)
        real = line % 8 < 4
        we[:, :nx] = jnp.where(real, cos, sin) * scale
        we[:, nx:] = jnp.where(real, -sin, cos) * scale

    y_shape, x_shape = (2 * nk, depth * yb), (2 * nx, 2 * nx)
    outs = [(y_shape, BF16)] * 4 + [(x_shape, BF16)] * 2
    outs += [((depth * 8, 2 * nk), F32)] * 2 + [((rows * 8, 2 * nx), F32)]
    oh, ol, ph, pl_, wh, wl, eo, ep, we = call(body, outs, where)
    return (oh, ol), (ph, pl_), (wh, wl), (eo, ep, we)


def past_sums(kernel, history):
    lags, comps, _, kyb, nx = kernel.shape

    def body(k_ref, h_ref, *out_refs):
        for comp in range(comps):
            line = pl.ds(comp * kyb, kyb)
            totals = [[None, None] for _ in range(STEPS)]
            for lag in range(1, lags):
                kr = k_ref[lag, comp, 0].astype(F32)
                ki = k_ref[lag, comp, 1].astype(F32)
                for step in range(STEPS):
                    if lag - 1 < step:
                        continue
                    hr = h_ref[lag - 1 - step, comp, 0].astype(F32)
                    hi = h_ref[lag - 1 - step, comp, 1].astype(F32)
                    for part, value in enumerate((kr * hr - ki * hi, kr * hi + ki * hr)):
                        old = totals[step][part]
                        totals[step][part] = value if old is None else old + value
            for step in range(STEPS):
                for part in range(2):
                    out_refs[step][line, pl.ds(part * nx, nx)] = totals[step][part]

    return call(body, [((comps * kyb, 2 * nx), F32)] * STEPS, kernel, history)


ROW_PARTS = (0, 3, 4)
COL_PARTS = (3, 1, 5)


def edge_weights(yb):
    line, lane = iota((8, yb), 0), iota((8, yb), 1)
    target = jnp.where(line < 2, line, yb - 4 + line)
    return jnp.where((lane == target) & (line < 4), 1.0, 0.0).astype(F32)


def inner_weights(yb):
    gap = iota((yb, yb), 0) - iota((yb, yb), 1)
    value = jnp.where(gap == 1, NEAR, 0.0) - jnp.where(gap == -1, NEAR, 0.0)
    return value + jnp.where(gap == 2, FAR, 0.0) - jnp.where(gap == -2, FAR, 0.0)


def outer_weights(yb, where_ref):
    line, lane = iota((8, yb), 0), iota((8, yb), 1)
    left_gap = jnp.where((line == 2) | (line == 3), line - 4 - lane, 99)
    right_gap = jnp.where(line < 2, yb + line - lane, 99)

    def value(gap):
        near = jnp.where(gap == 1, NEAR, 0.0) - jnp.where(gap == -1, NEAR, 0.0)
        return near + jnp.where(gap == 2, FAR, 0.0) - jnp.where(gap == -2, FAR, 0.0)

    left, right = value(left_gap), value(right_gap)
    odd = (where_ref[1] & 1) == 1
    return jnp.where(odd, left, right), jnp.where(odd, right, left)


def put_borders(planes, row_planes, col_planes, edge_ref, first_ref, last_ref):
    xb, yb = planes(row_planes[0]).shape
    for j, which in enumerate(row_planes):
        plane = planes(which)
        first_ref[2 * j : 2 * j + 2, :] = plane[:2]
        last_ref[2 * j : 2 * j + 2, :] = plane[xb - 2 :]
    stacked = jnp.concatenate([planes(which) for which in col_planes], axis=0)
    edge_ref[...] = dot6(edge_weights(yb), stacked, NT)


def row_deriv(pad_ref, plane, above, below):
    xb = plane.shape[0]
    pad_ref[8 : 8 + xb, :] = plane
    pad_ref[6:8, :] = above
    pad_ref[8 + xb : 10 + xb, :] = below
    near = pad_ref[9 : 9 + xb, :] - pad_ref[7 : 7 + xb, :]
    far = pad_ref[10 : 10 + xb, :] - pad_ref[6 : 6 + xb, :]
    return NEAR * near + FAR * far


def col_deriv(stacked, partner, across, partner_w, across_w):
    yb = stacked.shape[1]
    inner = dot6(stacked, inner_weights(yb), NN)
    return inner + (dot6(partner.T, partner_w, NN) + dot6(across.T, across_w, NN))


def depth_deriv(at, layer, layers):
    total = None
    for step, weight in ((1, NEAR), (-1, -NEAR), (2, FAR), (-2, -FAR)):
        if 0 <= layer + step < layers:
            term = weight * at(layer + step)
            total = term if total is None else total + term
    return total


def borders_shapes(layers, xb, yb):
    planes = 3 * layers
    return [((8, planes * xb), F32), ((2 * planes, yb), F32), ((2 * planes, yb), F32)]


def row_patch(above, below, xb):
    line, lane = iota((xb, 4), 0), iota((xb, 4), 1)
    gap = beyond(lane, xb) - line
    near = jnp.where(gap == 1, NEAR, 0.0) - jnp.where(gap == -1, NEAR, 0.0)
    weights = near + jnp.where(gap == 2, FAR, 0.0) - jnp.where(gap == -2, FAR, 0.0)
    total = weights[:, 0:1] * above[0:1] + weights[:, 1:2] * above[1:2]
    return total + (weights[:, 2:3] * below[0:1] + weights[:, 3:4] * below[1:2])


def plane_list(parts, layers):
    return [(p, l) for p in parts for l in range(layers)]


def first_borders(stress):
    _, layers, xb, yb = stress.shape

    def body(s_ref, *outs):
        rows, cols = plane_list(ROW_PARTS, layers), plane_list(COL_PARTS, layers)
        put_borders(lambda w: s_ref[w[0], w[1]], rows, cols, *outs)

    return call(body, borders_shapes(layers, xb, yb), stress)


def exchange_edges(edge):
    count = lax.axis_size("col")
    across = [(i, (i + 1 if i & 1 else i - 1) % count) for i in range(count)]
    return partner_perm(edge), lax.ppermute(edge, "col", across)


def exchange(borders):
    edge, first, last = borders
    above = shift_perm(last, "row", 1)
    below = shift_perm(first, "row", -1)
    return (above, below, *exchange_edges(edge))


DEPTH_PARTS = (4, 5, 2)


def inner_force(stress, comps):
    _, layers, xb, yb = stress.shape

    def body(s_ref, f_ref, pad):
        none = jnp.zeros((2, yb), F32)
        stacked = jnp.concatenate(
            [s_ref[p, l] for p, l in plane_list(COL_PARTS, layers)], axis=0
        )
        along_y = dot6(stacked, inner_weights(yb), NN)
        for comp in range(comps):
            for layer in range(layers):
                j = comp * layers + layer
                force = row_deriv(pad.at[j], s_ref[ROW_PARTS[comp], layer], none, none)
                force = force + along_y[j * xb : (j + 1) * xb]
                force = force + depth_deriv(lambda l: s_ref[DEPTH_PARTS[comp], l], layer, layers)
                f_ref[comp, layer] = force

    return call(
        body, [((comps, layers, xb, yb), F32)], stress,
        scratch=[pltpu.VMEM((comps * layers, xb + 16, yb), F32)],
    )[0]


def push_top(velocity, inner, buoyancy, halo):
    comps, layers, xb, yb = inner.shape

    def body(v_ref, f_ref, b_ref, up, dn, lf, rt, lw, rw, top_ref):
        left_w, right_w = lw[...], rw[...]
        for comp in range(comps):
            j = comp * layers
            pair, lane = slice(2 * j, 2 * j + 2), slice(j * xb, (j + 1) * xb)
            patch = row_patch(up[pair, :], dn[pair, :], xb)
            patch = patch + dot6(lf[:, lane].T, left_w, NN) + dot6(rt[:, lane].T, right_w, NN)
            push = b_ref[0] * (f_ref[comp, 0] + patch)
            top_ref[comp * xb : (comp + 1) * xb, :] = v_ref[comp, 0] + push

    return call(body, [((comps * xb, yb), F32)], velocity, inner, buoyancy, *halo)[0]


def push_rest(velocity, inner, buoyancy, halo, top):
    comps, layers, xb, yb = inner.shape

    def body(v_ref, f_ref, b_ref, up, dn, lf, rt, lw, rw, top_ref, nv_ref, edge, first, last):
        left_w, right_w = lw[...], rw[...]
        along_y = dot6(lf[...].T, left_w, NN) + dot6(rt[...].T, right_w, NN)
        for comp in range(comps):
            nv_ref[comp, 0] = top_ref[comp * xb : (comp + 1) * xb, :]
            for layer in range(1, layers):
                j = comp * layers + layer
                pair = slice(2 * j, 2 * j + 2)
                patch = row_patch(up[pair, :], dn[pair, :], xb) + along_y[j * xb : (j + 1) * xb]
                push = b_ref[layer] * (f_ref[comp, layer] + patch)
                nv_ref[comp, layer] = v_ref[comp, layer] + push
        planes = plane_list(range(comps), layers)
        put_borders(lambda w: nv_ref[w[0], w[1]], planes, planes, edge, first, last)

    outs = [(inner.shape, F32)] + borders_shapes(layers, xb, yb)
    new, *borders = call(body, outs, velocity, inner, buoyancy, *halo, top)
    return new, borders


def push_velocity(velocity, stress, buoyancy, halo):
    comps, layers, xb, yb = velocity.shape

    def body(v_ref, s_ref, b_ref, up, dn, lf, rt, lw, rw, nv_ref, pad):
        stacked = jnp.concatenate(
            [s_ref[p, l] for p, l in plane_list(COL_PARTS, layers)], axis=0
        )
        along_y = col_deriv(stacked, lf[...], rt[...], lw[...], rw[...])
        for comp in range(comps):
            for layer in range(layers):
                j = comp * layers + layer
                pair = slice(2 * j, 2 * j + 2)
                force = row_deriv(pad.at[j], s_ref[ROW_PARTS[comp], layer], up[pair, :], dn[pair, :])
                force = force + along_y[j * xb : (j + 1) * xb]
                force = force + depth_deriv(lambda l: s_ref[DEPTH_PARTS[comp], l], layer, layers)
                nv_ref[comp, layer] = v_ref[comp, layer] + b_ref[layer] * force

    return call(
        body, [(velocity.shape, F32)], velocity, stress, buoyancy, *halo,
        scratch=[pltpu.VMEM((comps * layers, xb + 16, yb), F32)],
    )[0]


def push_stress(stress, velocity, lame, shear, halo, traction=None):
    comps, layers, xb, yb = velocity.shape

    def body(s_ref, v_ref, l_ref, m_ref, up, dn, lf, rt, lw, rw, *refs):
        stacked = jnp.concatenate(
            [v_ref[c, l] for c, l in plane_list(range(comps), layers)], axis=0
        )
        if traction is None:
            ns_ref, *outs, pad = refs
        else:
            t_ref, ns_ref, face_ref, pad = refs
        along_y = col_deriv(stacked, lf[...], rt[...], lw[...], rw[...])
        skip = up.shape[0] - 2 * comps * layers
        for layer in range(layers):
            gx, gy, gz = [], [], []
            for comp in range(comps):
                j = comp * layers + layer
                pair = slice(skip + 2 * j, skip + 2 * j + 2)
                gx.append(row_deriv(pad.at[j], v_ref[comp, layer], up[pair, :], dn[pair, :]))
                gy.append(along_y[j * xb : (j + 1) * xb])
                gz.append(depth_deriv(lambda l: v_ref[comp, l], layer, layers))
            lam, mu = l_ref[layer], m_ref[layer]
            spread = lam * (gx[0] + gy[1] + gz[2])
            twice = 2.0 * mu
            old = [s_ref[part, layer] for part in range(6)]
            if traction is not None and layer == 0:
                for comp, part in enumerate(DEPTH_PARTS):
                    old[part] = old[part] + t_ref[comp * xb : (comp + 1) * xb, :]
            ns_ref[0, layer] = old[0] + spread + twice * gx[0]
            ns_ref[1, layer] = old[1] + spread + twice * gy[1]
            ns_ref[2, layer] = old[2] + spread + twice * gz[2]
            ns_ref[3, layer] = old[3] + mu * (gy[0] + gx[1])
            ns_ref[4, layer] = old[4] + mu * (gz[0] + gx[2])
            ns_ref[5, layer] = old[5] + mu * (gz[1] + gy[2])
        if traction is None:
            rows, cols = plane_list(ROW_PARTS, layers), plane_list(COL_PARTS, layers)
            put_borders(lambda w: ns_ref[w[0], w[1]], rows, cols, *outs)
        else:
            for comp, part in enumerate(DEPTH_PARTS):
                face_ref[comp * xb : (comp + 1) * xb, :] = ns_ref[part, 0]

    args = [stress, velocity, lame, shear, *halo] + ([] if traction is None else [traction])
    outs = [(stress.shape, F32)]
    outs += borders_shapes(layers, xb, yb) if traction is None else [((comps * xb, yb), F32)]
    new, *borders = call(
        body, outs, *args,
        scratch=[pltpu.VMEM((comps * layers, xb + 16, yb), F32)],
    )
    return new, borders


def total_of(refs):
    total = refs[0][...]
    for ref in refs[1:]:
        total = total + ref[...]
    return total


def top_after(pieces, velocity, buoyancy):
    comps, _, xb, yb = velocity.shape
    height = pieces[0].shape[0]

    def body(v_ref, b_ref, *refs):
        *piece_refs, sum_ref, face_ref, pad = refs
        total = total_of(piece_refs)
        sum_ref[...] = total
        main = comps * xb
        force = row_deriv(pad, total[:xb], total[main : main + 2], total[main + 2 : main + 4])
        side = total[main : main + 8, :xb].T
        line, lane = iota((8, yb), 0), iota((8, yb), 1)
        gap = jnp.where(line >= 4, beyond(line - 4, yb) - lane, 99)
        near = jnp.where(gap == 1, NEAR, 0.0) - jnp.where(gap == -1, NEAR, 0.0)
        outer = near + jnp.where(gap == 2, FAR, 0.0) - jnp.where(gap == -2, FAR, 0.0)
        force = force + (dot6(total[xb : 2 * xb], inner_weights(yb), NN) + dot6(side, outer, NN))
        for comp in range(comps - 1):
            face_ref[comp * xb : (comp + 1) * xb, :] = v_ref[comp, 0]
        face_ref[(comps - 1) * xb :, :] = v_ref[comps - 1, 0] + b_ref[0] * force

    return call(
        body, [((height, yb), F32), ((comps * xb, yb), F32)], velocity, buoyancy, *pieces,
        scratch=[pltpu.VMEM((xb + 16, yb), F32)],
    )


def finish_velocity(velocity, buoyancy, traction, face):
    comps, layers, xb, yb = velocity.shape

    def body(v_ref, b_ref, t_ref, f_ref, nv_ref, edge, first, last):
        for comp in range(comps):
            push = t_ref[comp * xb : (comp + 1) * xb, :]
            for layer in range(layers):
                new = v_ref[comp, layer]
                if layer == 0 and comp == comps - 1:
                    new = f_ref[comp * xb :, :]
                if layer in (1, 2):
                    weight = -NEAR if layer == 1 else -FAR
                    new = new + b_ref[layer] * (weight * push)
                nv_ref[comp, layer] = new
        planes = plane_list(range(comps), layers)
        put_borders(lambda w: nv_ref[w[0], w[1]], planes, planes, edge, first, last)

    outs = [(velocity.shape, F32)] + borders_shapes(layers, xb, yb)
    new, *borders = call(body, outs, velocity, buoyancy, traction, face)
    return new, borders


def add_traction(stress, faces, pieces):
    xb, yb = stress.shape[2:]
    comps = len(DEPTH_PARTS)

    def body(s_ref, f_ref, *refs):
        *piece_refs, ns_ref, new_ref, sems = refs
        new_ref[...] = f_ref[...] + total_of(piece_refs)
        copies = [
            pltpu.make_async_copy(
                new_ref.at[pl.ds(comp * xb, xb)], ns_ref.at[part, 0], sems.at[comp]
            )
            for comp, part in enumerate(DEPTH_PARTS)
        ]
        for copy in copies:
            copy.start()
        for copy in copies:
            copy.wait()

    anywhere = pl.BlockSpec(memory_space=pl.ANY)
    inside = pl.BlockSpec(memory_space=pltpu.VMEM)
    return pl.pallas_call(
        body,
        name="traction",
        out_shape=jax.ShapeDtypeStruct(stress.shape, F32),
        in_specs=[anywhere] + [inside] * (1 + len(pieces)),
        out_specs=anywhere,
        scratch_shapes=[pltpu.VMEM((comps * xb, yb), F32), pltpu.SemaphoreType.DMA((comps,))],
        input_output_aliases={0: 0},
        compiler_params=pltpu.CompilerParams(vmem_limit_bytes=VMEM_LIMIT),
        cost_estimate=pl.CostEstimate(
            flops=0, bytes_accessed=8 * comps * xb * yb, transcendentals=0
        ),
    )(stress, faces, *pieces)


def part_forward(blocks, table, dims, after=()):
    rows, _, xb, _, kyb = dims
    nk = rows * kyb
    comps = blocks[0].shape[0] // xb

    def body(*refs):
        hi, lo, out = refs[-3:]
        data = jnp.concatenate([ref[...] for ref in refs[:-3]], axis=1)
        total = dot3((hi[...], lo[...]), split(data), NT)
        for s in range(rows):
            for comp in range(comps):
                lane = slice(comp * xb, (comp + 1) * xb)
                real = total[s * kyb : (s + 1) * kyb, lane]
                imag = total[nk + s * kyb : nk + (s + 1) * kyb, lane]
                at = (s * comps + comp) * kyb
                out[at : at + kyb, :] = jnp.concatenate([real, imag], axis=1)

    return call(body, [((rows * comps * kyb, 2 * xb), F32)], *blocks, *table, after=after)[0]


def join(mine, other, first, last, dims):
    rows = dims[0]
    height, extra = mine.shape[0] // rows, first.shape[0]
    riders = {1: 1, rows - 1: 0}

    def body(a_ref, b_ref, *refs):
        borders, outs = refs[:2], refs[2:]
        for s, out in enumerate(outs):
            span = slice(s * height, (s + 1) * height)
            out[:height, :] = a_ref[span, :] + b_ref[span, :]
            if s in riders:
                out[height:, :] = borders[riders[s]][...]

    outs = [((height + (extra if s in riders else 0), mine.shape[1]), F32) for s in range(rows)]
    return call(body, outs, mine, other, first, last)


def convolve(blocks, table, past, kernel, before, dims, side=None):
    rows, _, xb, _, kyb = dims
    nx = rows * xb
    comps = blocks[0].shape[0] // kyb
    step = len(before)

    def body(*refs):
        if side is not None:
            side_ref, *refs = refs
        ins, outs = refs[: rows + 4 + step], refs[rows + 4 + step :]
        wide = (ins[rows][...], ins[rows + 1][...])
        past_ref, k_ref, olds = ins[rows + 2], ins[rows + 3], ins[rows + 4 :]
        data = jnp.concatenate([ref[: comps * kyb, :] for ref in ins[:rows]], axis=1)
        spec = dot3(split(data), wide, NN)
        spec_ref = outs[0]
        loads = []
        for comp in range(comps):
            line = slice(comp * kyb, (comp + 1) * kyb)
            now = (spec[line, :nx], spec[line, nx:])
            spec_ref[comp, 0] = now[0]
            spec_ref[comp, 1] = now[1]
            real, imag = past_ref[line, :nx], past_ref[line, nx:]
            terms = [now] + [(old[comp, 0], old[comp, 1]) for old in reversed(olds)]
            for lag, (sr, si) in enumerate(terms):
                kr, ki = k_ref[lag, comp, 0].astype(F32), k_ref[lag, comp, 1].astype(F32)
                real = real + (kr * sr - ki * si)
                imag = imag + (kr * si + ki * sr)
            loads.append(jnp.concatenate([real, imag], axis=1))
        back = dot3(split(jnp.concatenate(loads, axis=0)), wide, NT)
        if side is not None:
            halo = dot6(side_ref[...], loads[0], NT)
        for s, out in enumerate(outs[1:]):
            out[: comps * kyb, :] = back[:, s * 2 * xb : (s + 1) * 2 * xb]
            if side is not None:
                out[comps * kyb :, :] = jnp.zeros((8, 2 * xb), F32)
                out[comps * kyb :, :kyb] = halo[8 * s : 8 * s + 8]

    spec_shape = (comps, 2, kyb, nx)
    height = comps * kyb + (0 if side is None else 8)
    outs = [(spec_shape, F32)] + [((height, 2 * xb), F32)] * rows
    args = ([] if side is None else [side]) + [*blocks, *table, past, kernel, *before]
    spec, *pieces = call(body, outs, *args)
    return spec, pieces


def collect(spectra):
    def body(*refs):
        *ins, out = refs
        for n, ref in enumerate(ins):
            out[n] = ref[...]

    return call(body, [((len(spectra),) + spectra[0].shape, F32)], *spectra)[0]


def turn(blocks, dims, comps, after):
    rows, _, xb, _, kyb = dims
    main, wide = comps * xb, 2 * rows * kyb
    sides = blocks[0].shape[0] > comps * kyb

    def body(*refs):
        *blocks, out = refs
        for comp in range(comps):
            line = slice(comp * kyb, (comp + 1) * kyb)
            flat = jnp.concatenate([ref[line, :] for ref in blocks], axis=0).T
            out[comp * xb : (comp + 1) * xb, :] = jnp.concatenate([flat[:xb], flat[xb:]], axis=1)
        if sides:
            low = comps * kyb
            parts = [ref[low + 4 * p : low + 4 * p + 4, :kyb] for p in range(2) for ref in blocks]
            out[main : main + 8, :] = jnp.zeros((8, wide), F32)
            out[main : main + 4, :] = jnp.concatenate(parts, axis=1)

    return call(body, [((main + (8 if sides else 0), wide), F32)], *blocks, after=after)[0]


def y_inverse(d_ref, hi, lo, dims, side_ref):
    xb, yb, depth = dims[2], dims[3], dims[1] // 2
    total = dot3(split(d_ref[...]), (hi[...], lo[...]), NN)
    if side_ref is None:
        return total
    beside = dot6(side_ref[...], d_ref[xb : 2 * xb, :], NT)
    gap = jnp.zeros((8, yb - xb), F32)
    parts = [jnp.concatenate([beside[8 * t : 8 * t + 8], gap], axis=1) for t in range(depth)]
    main = total.shape[0] - 8
    return jnp.concatenate([total[:main], total[main:] + jnp.concatenate(parts, axis=1)], axis=0)


def part_inverse(data, table, dims, side=None):
    def body(d_ref, hi, lo, *refs):
        out = refs[-1]
        out[...] = y_inverse(d_ref, hi, lo, dims, refs[0] if side is not None else None)

    shape = (data.shape[0], dims[1] // 2 * dims[3])
    extra = [] if side is None else [side]
    return call(body, [(shape, F32)], data, *table, *extra)[0]


def rest_inverse(mine, data, table, dims, side=None):
    cols, yb = dims[1], dims[3]

    def body(m_ref, d_ref, hi, lo, *refs):
        side_ref, outs = (None, refs) if side is None else (refs[0], refs[1:])
        total = m_ref[...] + y_inverse(d_ref, hi, lo, dims, side_ref)
        for t, out in enumerate(outs):
            out[...] = total[:, t * yb : (t + 1) * yb]

    outs = [((mine.shape[0], yb), F32)] * (cols // 2)
    extra = [] if side is None else [side]
    return call(body, outs, mine, data, *table, *extra)


def in_turn(blocks):
    moved = []
    for t, block in enumerate(blocks, 1):
        moved.append(depth_perm(block, t))
    return moved


def gather_depth(block):
    return [block] + in_turn([block] * (lax.axis_size("col") // 2 - 1))


def forward(faces, borders, tables_, dims):
    mine, other = tables_[:2]
    edge, first, last = borders
    sent = part_forward(faces, other, dims, after=(first,))
    came = partner_perm(sent)
    kept = part_forward(faces, mine, dims)
    pieces = join(kept, came, first, last, dims)
    pieces = pieces[:1] + [shift_perm(pieces[s], "row", s) for s in range(1, dims[0])]
    beside = exchange_edges(edge)
    return pieces, (pieces[1], pieces[-1], *beside)


def inverse(pieces, tables_, dims, comps, last, after):
    mine, other, _, (side_mine, side_other, _) = tables_
    rows, _ = dims[:2]
    pieces = pieces[:1] + [shift_perm(pieces[s], "row", -s) for s in range(1, rows)]
    flat = turn(pieces, dims, comps, after)
    flat_other = partner_perm(flat)
    total = part_inverse(flat, mine, dims, None if last else side_mine)
    pieces = rest_inverse(total, flat_other, other, dims, None if last else side_other)
    return pieces[:1] + in_turn(pieces[1:])


def on_device(velocity, stress, buoyancy, lame, shear, kernel, history):
    rows, cols = lax.axis_size("row"), lax.axis_size("col")
    xb, yb = velocity.shape[2:]
    kyb = kernel.shape[3]
    dims = (rows, cols, xb, yb, kyb)
    where = jnp.stack([lax.axis_index("row"), lax.axis_index("col")]).astype(jnp.int32)

    halo = exchange(first_borders(stress))
    inner = inner_force(stress, velocity.shape[0])
    weights = outer_weights(yb, where)
    halo = (*halo, *weights)
    top = push_top(velocity, inner, buoyancy, halo)
    faces = gather_depth(top)
    tables_ = tables(where, dims)
    past = past_sums(kernel, history)
    recent = kernel[:STEPS]
    velocity, borders = push_rest(velocity, inner, buoyancy, halo, top)
    spectra = []
    traction = None
    for step in range(STEPS):
        last = step == STEPS - 1
        pieces, halo = forward(faces, borders, tables_, dims)
        halo = (*halo, *weights)
        side = None if last else tables_[3][2]
        spec, pieces = convolve(
            pieces, tables_[2], past[step], recent, spectra, dims, side
        )
        spectra.append(spec)
        stress, next_borders = push_stress(stress, velocity, lame, shear, halo, traction)
        after = () if last else (next_borders[1],)
        if not last:
            halo = (*exchange(next_borders), *weights)
        pieces = inverse(pieces, tables_, dims, recent.shape[1], last, after)
        if last:
            break
        velocity = push_velocity(velocity, stress, buoyancy, halo)
        traction, top = top_after(pieces, velocity, buoyancy)
        faces = gather_depth(top)
        velocity, borders = finish_velocity(velocity, buoyancy, traction, top)
    spectra = collect(spectra)
    stress = add_traction(stress, *next_borders, pieces)
    return (velocity, stress, spectra)


def solution(mesh):
    return jax.shard_map(
        on_device,
        mesh=mesh,
        in_specs=(
            P(None, None, "row", "col"),
            P(None, None, "row", "col"),
            P(None, "row", "col"),
            P(None, "row", "col"),
            P(None, "row", "col"),
            P(None, None, None, ("row", "col"), None),
            P(None, None, None, ("row", "col"), None),
        ),
        out_specs=(
            P(None, None, "row", "col"),
            P(None, None, "row", "col"),
            P(None, None, None, ("row", "col"), None),
        ),
        check_vma=False,
    )
```
